32 devices in a mesh: frame: 16 (over z, x, core), batch: 2 (over y).
Axes of the slice: x: 2, y: 2, z: 4, core: 2. Of those that a mesh axis runs over, the one named last changes fastest.
Arguments:
- latents: bfloat16 [32, 256, 640], P(('batch', 'frame')), parts along dimension 0, may hold values from -6 to 6
- query_space: bfloat16 [640, 640], replicated, may hold values from -8 to 8
- key_space: bfloat16 [640, 640], replicated, may hold values from -8 to 8
- value_space: bfloat16 [640, 640], replicated, may hold values from -0.25 to 0.25
- out_space: bfloat16 [640, 640], replicated, may hold values from -0.25 to 0.25
- query_time: bfloat16 [640, 640], replicated, may hold values from -8 to 8
- key_time: bfloat16 [640, 640], replicated, may hold values from -8 to 8
- value_time: bfloat16 [640, 640], replicated, may hold values from -0.25 to 0.25
- out_time: bfloat16 [640, 640], replicated, may hold values from -0.25 to 0.25
- position_bias: float32 [8, 32], replicated, may hold values from -4 to 4
- bucket_table: int32 [257], replicated, may hold values from 0 to 31, as said below
Outputs:
- edited: bfloat16 [32, 256, 640], P(('batch', 'frame')), parts along dimension 0
The draws below stay inside these ranges and needn't reach their ends.
There are 2 independent parts, one for each index of `batch`. The reference program is written for one: setup_inputs(seed, part) draws one part's arguments, and reference() takes and returns one part's arrays. A program takes and returns all parts, laid end to end along the dimension named above; an argument that names none is the same for every part. Nothing has to cross between parts.
Inputs may be any that keep to these rules, and one draw needn't show every extreme that they name: `bucket_table`: entry 128 + d is the bucket of frame offset d; offsets 0 and above take ids below 16, never falling as d grows, offset 0 takes id 0; negative offsets take the other ids, never falling as -d grows.
All inputs are finite; a program needn't handle non-finite values.
Results may differ from the reference program's by a relative error of at most 0.012.
Values may be sent and summed in bfloat16 or wider, within the bound.
A program may use at most 64 MiB of HBM per device.

```python
import math
import jax
import jax.numpy as jnp
from jax import lax

D = 640
HEADS = 8
HEAD_DIM = 80
BUCKETS = 32
MAX_DIST = 128
POS = 256
FRAMES = 16


def paired_weights(key, marker):
    base = jax.random.fold_in(key, marker)
    query = jax.random.normal(jax.random.fold_in(base, 1), (D, D), jnp.float32) * D ** (-0.5)
    other = jax.random.normal(jax.random.fold_in(base, 2), (D, D), jnp.float32) * D ** (-0.5)
    return (jnp.clip(query, -8.0, 8.0), jnp.clip(other, -8.0, 8.0))


def draw_query_space(key, part):
    return paired_weights(key, 11)[0].astype(jnp.bfloat16)


def draw_key_space(key, part):
    return paired_weights(key, 11)[1].astype(jnp.bfloat16)


def draw_query_time(key, part):
    return paired_weights(key, 12)[0].astype(jnp.bfloat16)


def draw_key_time(key, part):
    return paired_weights(key, 12)[1].astype(jnp.bfloat16)


def one_side(key):
    half = BUCKETS // 2
    shuffled = jax.random.permutation(key, MAX_DIST - 1) + 1
    cutoffs = shuffled[:half - 1]
    distance = jnp.arange(MAX_DIST + 1, dtype=jnp.int32)
    return jnp.sum((cutoffs[None, :] <= distance[:, None]).astype(jnp.int32), axis=1).astype(jnp.int32)


def draw_bucket_table(key, part):
    half = BUCKETS // 2
    upper = one_side(jax.random.fold_in(key, 21))
    lower = one_side(jax.random.fold_in(key, 22)) + half
    return jnp.concatenate([lower[1:][::-1], upper]).astype(jnp.int32)


def block_scale(rng, dims, split, smallest, top_value):
    level = 1.0
    for dim, shards_of in split:
        heights = jax.random.uniform(jax.random.fold_in(jax.random.fold_in(rng, 6), dim), (shards_of,), jnp.float32, smallest / len(split), top_value / len(split))
        level = level * jnp.repeat(jnp.exp(heights), dims[dim] // shards_of).reshape((-1,) + (1,) * (len(dims) - 1 - dim))
    return level


def bell_draw(own_key, extent, scale, most, shards=(), held_as=jnp.bfloat16):
    entries = scale * jax.random.normal(own_key, extent, jnp.float32)
    if shards:
        entries = entries * block_scale(own_key, extent, shards, -0.22, 0.18)
    return jnp.clip(entries, -most, most).astype(held_as)


def setup_inputs(seed: int = 0, part: int = 0) -> dict:
    streams_of = jax.random.split(jax.random.key(seed), 12)
    part_keys = jax.random.split(jax.random.fold_in(streams_of[11], part), 12)
    latents = bell_draw(part_keys[0], (FRAMES, POS, D), 1.0, 6.0, ((0, 16),))
    query_space = draw_query_space(jax.random.fold_in(streams_of[11], 71), part)
    key_space = draw_key_space(jax.random.fold_in(streams_of[11], 71), part)
    value_space = bell_draw(streams_of[3], (D, D), D ** -0.5, 0.25)
    out_space = bell_draw(streams_of[4], (D, D), D ** -0.5, 0.25)
    query_time = draw_query_time(jax.random.fold_in(streams_of[11], 71), part)
    key_time = draw_key_time(jax.random.fold_in(streams_of[11], 71), part)
    value_time = bell_draw(streams_of[7], (D, D), D ** -0.5, 0.25)
    out_time = bell_draw(streams_of[8], (D, D), D ** -0.5, 0.25)
    position_bias = bell_draw(streams_of[9], (HEADS, BUCKETS), 1.0, 4.0, (), jnp.float32)
    bucket_table = draw_bucket_table(jax.random.fold_in(streams_of[11], 71), part)
    return {"latents": latents, "query_space": query_space, "key_space": key_space, "value_space": value_space, "out_space": out_space, "query_time": query_time, "key_time": key_time, "value_time": value_time, "out_time": out_time, "position_bias": position_bias, "bucket_table": bucket_table}


EPS = 1e-05

def normalize(values):
    floats = values.astype(jnp.float32)
    average = lax.optimization_barrier(jnp.mean(floats, axis=-1, keepdims=True))
    centred = floats - average
    spread = lax.optimization_barrier(jnp.mean(centred * centred, axis=-1, keepdims=True))
    return (centred * lax.rsqrt(spread + EPS)).astype(jnp.bfloat16)

def project(rows, weight):
    lead = rows.shape[:-1]
    flat = rows.reshape(-1, rows.shape[-1])
    result = jnp.dot(flat, weight, preferred_element_type=jnp.float32)
    return result.reshape(lead + (weight.shape[1],)).astype(jnp.bfloat16)

def softmax_rows(scores):
    highest = lax.optimization_barrier(jnp.max(scores, axis=-1, keepdims=True))
    powered = jnp.exp(scores - highest)
    return (powered / lax.optimization_barrier(jnp.sum(powered, axis=-1, keepdims=True))).astype(jnp.bfloat16)

def reference(latents, query_space, key_space, value_space, out_space, query_time, key_time, value_time, out_time, position_bias, bucket_table):
    frames, places, channels = latents.shape
    factor = 1.0 / math.sqrt(HEAD_DIM)
    normed = normalize(latents)
    space_q = project(normed, query_space)
    space_k = project(normed, key_space)
    space_v = project(normed, value_space)
    prior_k = jnp.concatenate([space_k[:1], space_k[:-1]], axis=0)
    prior_v = jnp.concatenate([space_v[:1], space_v[:-1]], axis=0)

    def spatial(inputs):
        queries, keys_prior, values_prior = inputs
        key_rows = jnp.concatenate([space_k[0], keys_prior], axis=0).reshape(2 * places, HEADS, HEAD_DIM).astype(jnp.float32)
        value_rows = jnp.concatenate([space_v[0], values_prior], axis=0).reshape(2 * places, HEADS, HEAD_DIM).astype(jnp.float32)
        query_rows = queries.reshape(places, HEADS, HEAD_DIM).astype(jnp.float32)
        scores = jnp.einsum('qhe,khe->hqk', query_rows, key_rows) * factor
        weights = softmax_rows(scores)
        mixed = jnp.einsum('hqk,khe->qhe', weights.astype(jnp.float32), value_rows)
        return mixed.reshape(places, channels).astype(jnp.bfloat16)
    space_mix = lax.map(spatial, (space_q, prior_k, prior_v))
    after_space = (latents.astype(jnp.float32) + jnp.dot(space_mix.reshape(-1, channels), out_space, preferred_element_type=jnp.float32).reshape(frames, places, channels)).astype(jnp.bfloat16)
    normed_two = normalize(after_space)
    time_q = jnp.swapaxes(project(normed_two, query_time), 0, 1)
    time_k = jnp.swapaxes(project(normed_two, key_time), 0, 1)
    time_v = jnp.swapaxes(project(normed_two, value_time), 0, 1)
    limit = (bucket_table.shape[0] - 1) // 2
    bias_rows = position_bias[:, bucket_table]
    order = jnp.arange(frames, dtype=jnp.int32)
    offsets = jnp.clip(order[None, :] - order[:, None], -limit, limit) + limit
    bias = bias_rows[:, offsets]

    def temporal(inputs):
        queries, keys, values = inputs
        query_rows = queries.reshape(frames, HEADS, HEAD_DIM).astype(jnp.float32)
        key_rows = keys.reshape(frames, HEADS, HEAD_DIM).astype(jnp.float32)
        value_rows = values.reshape(frames, HEADS, HEAD_DIM).astype(jnp.float32)
        scores = jnp.einsum('ihe,jhe->hij', query_rows, key_rows) * factor + bias
        weights = softmax_rows(scores)
        mixed = jnp.einsum('hij,jhe->ihe', weights.astype(jnp.float32), value_rows)
        return mixed.reshape(frames, channels).astype(jnp.bfloat16)
    time_mix = jnp.swapaxes(lax.map(temporal, (time_q, time_k, time_v)), 0, 1)
    edited = after_space.astype(jnp.float32) + jnp.dot(time_mix.reshape(-1, channels), out_time, preferred_element_type=jnp.float32).reshape(frames, places, channels)
    return edited.astype(jnp.bfloat16)
```

```python
import functools
import math

import jax
import jax.numpy as jnp
from jax import lax
from jax.experimental import pallas as pl
from jax.experimental.pallas import tpu as pltpu
from jax.sharding import PartitionSpec as P

HEADS = 8
HEAD_DIM = 80


EPS = 1e-05


def from_behind(x, axis, by):
    size = lax.axis_size(axis)
    pairs = [(i, i + by) for i in range(size) if 0 <= i + by < size]
    return lax.ppermute(x, axis, pairs)


def spread_2(block, axis, source):
    block = jnp.where(lax.axis_index(axis) == source, block, jnp.zeros_like(block))
    return lax.psum(block, axis)


def normalize(values):
    floats = values.astype(jnp.float32)
    average = jnp.mean(floats, axis=-1, keepdims=True)
    centred = floats - average
    spread = jnp.mean(centred * centred, axis=-1, keepdims=True)
    return (centred * lax.rsqrt(spread + EPS)).astype(jnp.bfloat16)


def project(rows, weight):
    lead = rows.shape[:-1]
    flat = rows.reshape(-1, rows.shape[-1])
    result = jnp.dot(flat, weight, preferred_element_type=jnp.float32)
    return result.reshape(lead + (weight.shape[1],)).astype(jnp.bfloat16)


def softmax_rows(scores):
    highest = jnp.max(scores, axis=-1, keepdims=True)
    powered = jnp.exp(scores - highest)
    return (powered / jnp.sum(powered, axis=-1, keepdims=True)).astype(jnp.bfloat16)


def temporal_attend(time_q, time_k, time_v, bias_rows):
    frames, places, channels = time_q.shape
    factor = 1.0 / math.sqrt(HEAD_DIM)
    block_rows = math.gcd(frames, 512)
    blocks = frames // block_rows
    limit = (bias_rows.shape[1] - 1) // 2
    key_rows = time_k.reshape(frames, places, HEADS, HEAD_DIM)
    value_rows = time_v.reshape(frames, places, HEADS, HEAD_DIM)
    columns = jnp.arange(frames, dtype=jnp.int32)

    def one_block(begin_row):
        query_rows = time_q.reshape(block_rows, places, HEADS, HEAD_DIM)
        row_ids = begin_row + jnp.arange(block_rows, dtype=jnp.int32)
        offsets = jnp.clip(columns[None, :] - row_ids[:, None], -limit, limit) + limit
        bias = bias_rows[:, offsets]
        scores = (
            jnp.einsum("iphe,jphe->phij", query_rows, key_rows, preferred_element_type=jnp.float32)
            * factor
            + bias[None]
        )
        weights = softmax_rows(scores)
        mixed = jnp.einsum(
            "phij,jphe->iphe", weights, value_rows, preferred_element_type=jnp.float32
        )
        return mixed.astype(jnp.bfloat16).reshape(block_rows, places, channels)

    results = lax.map(one_block, jnp.arange(blocks, dtype=jnp.int32) * block_rows)
    return results.reshape(frames, places, channels)


def squeeze_items(rows):
    return rows.reshape(rows.shape[0], rows.shape[2], rows.shape[3])


def body(
    latents,
    query_space,
    key_space,
    value_space,
    out_space,
    query_time,
    key_time,
    value_time,
    out_time,
    position_bias,
    bucket_table,
):
    frames, places, channels = latents.shape
    factor = 1.0 / math.sqrt(HEAD_DIM)
    normed = normalize(latents)
    space_q = project(normed, query_space)
    space_k = project(normed, key_space)
    space_v = project(normed, value_space)
    prior_pair = from_behind(jnp.stack([space_k[-1], space_v[-1]]), "frame", 1)
    first_pair = spread_2(jnp.stack([space_k[0], space_v[0]]), "frame", 0)
    prior_keys, prior_values = (prior_pair[0], prior_pair[1])
    first_keys, first_values = (first_pair[0], first_pair[1])
    is_first = lax.axis_index("frame") == 0
    prior_keys = jnp.where(is_first, first_keys, prior_keys)
    prior_values = jnp.where(is_first, first_values, prior_values)
    before_keys = jnp.concatenate([prior_keys[None], space_k[:-1]], axis=0)
    before_values = jnp.concatenate([prior_values[None], space_v[:-1]], axis=0)
    key_rows = jnp.concatenate([first_keys[None], before_keys], axis=1)
    value_rows = jnp.concatenate([first_values[None], before_values], axis=1)
    query_rows = space_q.reshape(frames, places, HEADS, HEAD_DIM)
    key_rows = key_rows.reshape(frames, 2 * places, HEADS, HEAD_DIM)
    value_rows = value_rows.reshape(frames, 2 * places, HEADS, HEAD_DIM)
    scores = (
        jnp.einsum("fqhe,fkhe->fhqk", query_rows, key_rows, preferred_element_type=jnp.float32)
        * factor
    )
    weights = softmax_rows(scores)
    space_mix = jnp.einsum(
        "fhqk,fkhe->fqhe", weights, value_rows, preferred_element_type=jnp.float32
    ).astype(jnp.bfloat16)
    space_out = jnp.dot(
        space_mix.reshape(-1, channels), out_space, preferred_element_type=jnp.float32
    ).reshape(frames, places, channels)
    after_space = (latents.astype(jnp.float32) + space_out).astype(jnp.bfloat16)
    normed_two = normalize(after_space)
    onehot = (
        bucket_table[:, None] == jnp.arange(position_bias.shape[1], dtype=jnp.int32)[None, :]
    ).astype(jnp.float32)
    bias_rows = jnp.dot(position_bias, onehot.T, precision=lax.Precision.HIGHEST)
    owners = lax.axis_size("frame")
    share = places // owners
    flat_rows = squeeze_items(
        lax.all_to_all(
            normed_two.reshape(frames, owners, share, channels),
            "frame",
            split_axis=1,
            concat_axis=0,
            tiled=True,
        )
    )
    mixed = temporal_attend(
        project(flat_rows, query_time),
        project(flat_rows, key_time),
        project(flat_rows, value_time),
        bias_rows,
    )
    gathered_mix = mixed[:, None]
    time_mix = lax.all_to_all(
        gathered_mix, "frame", split_axis=0, concat_axis=1, tiled=True
    ).reshape(frames, places, channels)
    time_out = jnp.dot(
        time_mix.reshape(-1, channels), out_time, preferred_element_type=jnp.float32
    ).reshape(frames, places, channels)
    return (after_space.astype(jnp.float32) + time_out).astype(jnp.bfloat16)


AXIS = "frame"
MESH = pl.DeviceIdType.MESH
LANES = 128
FAR_BELOW = -1e30
LOG2E = 1.4426950408889634


def windows(channels):
    spans = []
    for head in range(HEADS):
        begin, end = head * HEAD_DIM, (head + 1) * HEAD_DIM
        low = begin // LANES * LANES
        high = min(-(-end // LANES) * LANES, channels)
        spans.append((low, high, begin - low, end - low))
    return spans


def attend(q_ref, k_ref, v_ref, rows, scale, bias_ref):
    channels = q_ref.shape[-1]
    tiles = [None] * (channels // LANES)
    for head, (low, high, begin, end) in enumerate(windows(channels)):
        lane = lax.broadcasted_iota(jnp.int32, (rows.size, high - low), 1)
        inside = (lane >= begin) & (lane < end)
        query = q_ref[rows, low:high]
        query = jnp.where(inside, query, jnp.zeros_like(query))
        scores = lax.dot_general(
            query, k_ref[:, low:high], (((1,), (1,)), ((), ())), preferred_element_type=jnp.float32
        )
        if bias_ref is None:
            highest = jnp.max(scores, axis=-1, keepdims=True)
            powered = jnp.exp2((scores - highest) * (scale * LOG2E))
        else:
            scores = scores * scale + bias_ref[head, rows, :]
            highest = jnp.max(scores, axis=-1, keepdims=True)
            powered = jnp.exp2((scores - highest) * LOG2E)
        total = jnp.sum(powered, axis=-1, keepdims=True)
        mixed = jnp.dot(
            powered.astype(jnp.bfloat16), v_ref[:, low:high], preferred_element_type=jnp.float32
        )
        mixed = mixed * (1.0 / total)
        for at in range(low, high, LANES):
            part = mixed[:, at - low : at - low + LANES]
            keep = inside[:, at - low : at - low + LANES]
            old = tiles[at // LANES]
            tiles[at // LANES] = part if old is None else jnp.where(keep, part, old)
    return jnp.concatenate([t.astype(jnp.bfloat16) for t in tiles], axis=1)


def norm_rows(floats):
    average = jnp.mean(floats, axis=-1, keepdims=True)
    centred = floats - average
    spread = jnp.mean(centred * centred, axis=-1, keepdims=True)
    return (centred * lax.rsqrt(spread + EPS)).astype(jnp.bfloat16)


def matmul(rows, weight):
    return jnp.dot(rows, weight, preferred_element_type=jnp.float32)


def block_kernel(
    n,
    share,
    lat,
    *refs,
):
    weights, refs = refs[:8], refs[8:]
    pos_bias, buckets, out = refs[:3]
    (
        x,
        w,
        first,
        prior,
        q,
        k,
        v,
        after,
        go,
        came,
        back_go,
        back_came,
        bias,
        x_sem,
        w_sem,
        prior_sems,
        a_send,
        b_send,
        c_send,
        first_recv,
        go_send,
        go_recv,
        back_send,
        back_recv,
    ) = refs[3:]
    me = lax.axis_index(AXIS)
    places, channels = x.shape
    scale = 1.0 / math.sqrt(HEAD_DIM)
    other = lax.rem(me + 1, n)

    barrier = pltpu.get_barrier_semaphore()

    @pl.loop(1, n)
    def _(step):
        pl.semaphore_signal(
            barrier, inc=1, device_id={AXIS: lax.rem(me + step, n)}, device_id_type=MESH
        )

    own = pltpu.make_async_copy(lat.at[0], x, x_sem)
    own.start()
    loads = [pltpu.make_async_copy(weights[i], w.at[i], w_sem.at[i]) for i in range(8)]
    for load in loads:
        load.start()

    onehot = (
        lax.broadcasted_iota(jnp.int32, (pos_bias.shape[1], 256), 0) == buckets[:, 0:256]
    ).astype(jnp.float32)
    by_offset = jnp.dot(
        pos_bias[...], onehot, precision=lax.Precision.HIGHEST, preferred_element_type=jnp.float32
    )
    limit = (buckets.shape[1] - 1) // 2
    wide = 2 * n * share
    pick = (
        lax.broadcasted_iota(jnp.int32, (256, wide), 0)
        == lax.broadcasted_iota(jnp.int32, (256, wide), 1) // share + (limit - (n - 1))
    ).astype(jnp.float32)
    spread = jnp.dot(
        by_offset, pick, precision=lax.Precision.HIGHEST, preferred_element_type=jnp.float32
    )
    same = lax.broadcasted_iota(jnp.int32, (share, n * share), 0) == lax.rem(
        lax.broadcasted_iota(jnp.int32, (share, n * share), 1), share
    )
    for i in range(n):
        begin = (n - 1 - i) * share
        line = spread[:, begin : begin + n * share]
        for head in range(HEADS):
            bias[head, i * share : (i + 1) * share, :] = jnp.where(
                same, line[head : head + 1, :], FAR_BELOW
            )

    pl.semaphore_wait(barrier, n - 1)

    def chunk(c):
        return lat.at[0, pl.ds(pl.multiple_of(c * share, share), share), :]

    def scatter(c):
        return pltpu.make_async_remote_copy(
            chunk(c), first.at[c], a_send.at[c], first_recv.at[c], {AXIS: c}, MESH
        )

    def gather(c, to):
        return pltpu.make_async_remote_copy(
            first.at[c], first.at[c], b_send.at[to], first_recv.at[c], {AXIS: to}, MESH
        )

    sibling = me + 1 - 2 * lax.rem(me, 2)

    def pair(c):
        return pltpu.make_async_remote_copy(
            first.at[c], first.at[c], c_send.at[c], first_recv.at[c], {AXIS: sibling}, MESH
        )

    send_prior = pltpu.make_async_remote_copy(
        lat.at[0], prior, prior_sems.at[0], prior_sems.at[1], {AXIS: other}, MESH
    )

    @pl.when(me == 0)
    def _():
        @pl.loop(1, n)
        def _(step):
            scatter(n - step).start()

    @pl.when(me < n - 1)
    def _():
        send_prior.start()

    own.wait()

    @pl.when(me == 0)
    def _():
        prior[...] = x[...]
        first[...] = x[...].reshape(n, share, channels)

    def took(c):
        pltpu.make_async_remote_copy(
            first.at[c], first.at[c], b_send.at[0], first_recv.at[c], {AXIS: other}, MESH
        ).wait_recv()

    @pl.when(me > 0)
    def _():
        took(me)

    @pl.loop(1, n // 2)
    def _(step):
        to = lax.rem(me + 2 * step, n)

        @pl.when(to != 0)
        def _():
            gather(me, to).start()

    @pl.when(sibling != 0)
    def _():
        pair(me).start()

    normed = norm_rows(x[...].astype(jnp.float32))
    loads[0].wait()
    q[...] = matmul(normed, w[0]).astype(jnp.bfloat16)

    @pl.loop(1, n // 2)
    def _(step):
        c = lax.rem(me + n - 2 * step, n)

        @pl.when(me > 0)
        def _():
            took(c)

        @pl.when(sibling != 0)
        def _():
            pair(c).start()

    @pl.when(me > 0)
    def _():
        pltpu.make_async_remote_copy(
            lat.at[0], prior, prior_sems.at[0], prior_sems.at[1], {AXIS: other}, MESH
        ).wait_recv()

    normed = norm_rows(prior[...].astype(jnp.float32))
    loads[1].wait()
    loads[2].wait()
    k[places:, :] = matmul(normed, w[1]).astype(jnp.bfloat16)
    v[places:, :] = matmul(normed, w[2]).astype(jnp.bfloat16)

    @pl.when(me > 0)
    def _():
        @pl.loop(0, n // 2)
        def _(step):
            took(2 * step + lax.rem(me + 1, 2))

    normed = norm_rows(first[...].reshape(places, channels).astype(jnp.float32))
    k[:places, :] = matmul(normed, w[1]).astype(jnp.bfloat16)
    v[:places, :] = matmul(normed, w[2]).astype(jnp.bfloat16)

    for i in range(3, 8):
        loads[i].wait()

    halves = 2
    size = places // halves

    def to_owner(to):
        return pltpu.make_async_remote_copy(
            go.at[to], came.at[me], go_send.at[to], go_recv.at[me], {AXIS: to}, MESH
        )

    def to_frame(to):
        return pltpu.make_async_remote_copy(
            back_go.at[to], back_came.at[me], back_send.at[to], back_recv.at[me], {AXIS: to}, MESH
        )

    def start_group(make, half):
        count = n // halves

        @pl.loop(0, count)
        def _(step):
            to = half * count + lax.rem(me + step, count)

            @pl.when(to != me)
            def _():
                make(to).start()

    def space_block(half):
        rows = pl.ds(pl.multiple_of(half * size, size), size)
        mix = attend(q, k, v, rows, scale, None)
        summed = x[rows, :].astype(jnp.float32) + matmul(mix, w[3])
        rounded = summed.astype(jnp.bfloat16)
        after[rows, :] = rounded
        go[pl.ds(half * (n // halves), n // halves)] = norm_rows(
            rounded.astype(jnp.float32)
        ).reshape(n // halves, share, channels)
        start_group(to_owner, half)

    pl.loop(0, halves)(space_block)

    came[pl.ds(me, 1)] = go[pl.ds(me, 1)]

    @pl.loop(1, n)
    def _(step):
        c = lax.rem(me + step, n)
        pltpu.make_async_remote_copy(
            came.at[c], came.at[c], go_send.at[c], go_recv.at[c], {AXIS: c}, MESH
        ).wait_recv()

    rows = came[...].reshape(n * share, channels)
    q[...] = matmul(rows, w[4]).astype(jnp.bfloat16)
    k[:places, :] = matmul(rows, w[5]).astype(jnp.bfloat16)
    v[:places, :] = matmul(rows, w[6]).astype(jnp.bfloat16)

    def time_block(half):
        rows = pl.ds(pl.multiple_of(half * size, size), size)
        mix = attend(q, k.at[:places], v.at[:places], rows, scale, bias)
        back_go[pl.ds(half * (n // halves), n // halves)] = mix.reshape(
            n // halves, share, channels
        )
        start_group(to_frame, half)

    pl.loop(0, halves)(time_block)

    back_came[pl.ds(me, 1)] = back_go[pl.ds(me, 1)]

    @pl.loop(1, n)
    def _(step):
        c = lax.rem(me + step, n)
        pltpu.make_async_remote_copy(
            back_came.at[c], back_came.at[c], back_send.at[c], back_recv.at[c], {AXIS: c}, MESH
        ).wait_recv()

    mix = back_came[...].reshape(places, channels)
    out[0] = (after[...].astype(jnp.float32) + matmul(mix, w[7])).astype(jnp.bfloat16)

    @pl.when(me == 0)
    def _():
        @pl.loop(1, n)
        def _(step):
            scatter(n - step).wait_send()

    @pl.when(me < n - 1)
    def _():
        send_prior.wait_send()

    @pl.loop(1, n // 2)
    def _(step):
        to = lax.rem(me + 2 * step, n)

        @pl.when(to != 0)
        def _():
            gather(me, to).wait_send()

    @pl.when(sibling != 0)
    def _():
        @pl.loop(0, n // 2)
        def _(step):
            pair(lax.rem(me + 2 * step, n)).wait_send()

    @pl.loop(1, n)
    def _(step):
        c = lax.rem(me + step, n)
        to_owner(c).wait_send()
        to_frame(c).wait_send()


def kernel_body(
    latents,
    query_space,
    key_space,
    value_space,
    out_space,
    query_time,
    key_time,
    value_time,
    out_time,
    position_bias,
    bucket_table,
):
    _, places, channels = latents.shape
    n = lax.axis_size(AXIS)
    share = places // n
    rows = n * share
    bf16 = jnp.bfloat16
    anywhere = pl.BlockSpec(memory_space=pl.ANY)
    vmem = pl.BlockSpec(memory_space=pltpu.VMEM)
    blocks = pltpu.VMEM((n, share, channels), bf16)
    plane = pltpu.VMEM((places, channels), bf16)
    dma = pltpu.SemaphoreType.DMA
    return pl.pallas_call(
        functools.partial(block_kernel, n, share),
        out_shape=jax.ShapeDtypeStruct(latents.shape, bf16),
        in_specs=[anywhere] * 9 + [vmem] * 2,
        out_specs=vmem,
        scratch_shapes=[
            plane,
            pltpu.VMEM((8, channels, channels), bf16),
            blocks,
            plane,
            plane,
            pltpu.VMEM((2 * places, channels), bf16),
            pltpu.VMEM((2 * places, channels), bf16),
            plane,
            blocks,
            blocks,
            blocks,
            blocks,
            pltpu.VMEM((HEADS, rows, rows), jnp.float32),
            dma,
            dma((8,)),
            dma((2,)),
            dma((n,)),
            dma((n,)),
            dma((n,)),
            dma((n,)),
            dma((n,)),
            dma((n,)),
            dma((n,)),
            dma((n,)),
        ],
        compiler_params=pltpu.CompilerParams(
            collective_id=0, has_side_effects=True, vmem_limit_bytes=48 * 1024 * 1024
        ),
    )(
        latents,
        query_space,
        key_space,
        value_space,
        out_space,
        query_time,
        key_time,
        value_time,
        out_time,
        position_bias,
        bucket_table.reshape(1, -1),
    )


def one_kernel(latents, *rest):
    frames, places, _ = latents.shape
    n = lax.axis_size(AXIS)
    limit = (rest[-1].shape[0] - 1) // 2
    fits = frames == 1 and n % 2 == 0 and places % (16 * n) == 0 and limit + n <= 256 and n <= limit
    return (kernel_body if fits else body)(latents, *rest)


def solution(mesh):
    in_specs = (P(("batch", "frame"), None, None), P(), P(), P(), P(), P(), P(), P(), P(), P(), P())
    out_specs = P(("batch", "frame"), None, None)
    return jax.shard_map(one_kernel, mesh=mesh, in_specs=in_specs, out_specs=out_specs, check_vma=False)
```

```python
import functools
import math

import jax
import jax.numpy as jnp
from jax import lax
from jax.experimental import pallas as pl
from jax.experimental.pallas import tpu as pltpu
from jax.sharding import PartitionSpec as P

HEADS = 8
HEAD_DIM = 80


EPS = 1e-05


def from_behind(x, axis, by):
    size = lax.axis_size(axis)
    pairs = [(i, i + by) for i in range(size) if 0 <= i + by < size]
    return lax.ppermute(x, axis, pairs)


def spread_2(block, axis, source):
    block = jnp.where(lax.axis_index(axis) == source, block, jnp.zeros_like(block))
    return lax.psum(block, axis)


def normalize(values):
    floats = values.astype(jnp.float32)
    average = jnp.mean(floats, axis=-1, keepdims=True)
    centred = floats - average
    spread = jnp.mean(centred * centred, axis=-1, keepdims=True)
    return (centred * lax.rsqrt(spread + EPS)).astype(jnp.bfloat16)


def project(rows, weight):
    lead = rows.shape[:-1]
    flat = rows.reshape(-1, rows.shape[-1])
    result = jnp.dot(flat, weight, preferred_element_type=jnp.float32)
    return result.reshape(lead + (weight.shape[1],)).astype(jnp.bfloat16)


def softmax_rows(scores):
    highest = jnp.max(scores, axis=-1, keepdims=True)
    powered = jnp.exp(scores - highest)
    return (powered / jnp.sum(powered, axis=-1, keepdims=True)).astype(jnp.bfloat16)


def temporal_attend(time_q, time_k, time_v, bias_rows):
    frames, places, channels = time_q.shape
    factor = 1.0 / math.sqrt(HEAD_DIM)
    block_rows = math.gcd(frames, 512)
    blocks = frames // block_rows
    limit = (bias_rows.shape[1] - 1) // 2
    key_rows = time_k.reshape(frames, places, HEADS, HEAD_DIM)
    value_rows = time_v.reshape(frames, places, HEADS, HEAD_DIM)
    columns = jnp.arange(frames, dtype=jnp.int32)

    def one_block(begin_row):
        query_rows = time_q.reshape(block_rows, places, HEADS, HEAD_DIM)
        row_ids = begin_row + jnp.arange(block_rows, dtype=jnp.int32)
        offsets = jnp.clip(columns[None, :] - row_ids[:, None], -limit, limit) + limit
        bias = bias_rows[:, offsets]
        scores = (
            jnp.einsum("iphe,jphe->phij", query_rows, key_rows, preferred_element_type=jnp.float32)
            * factor
            + bias[None]
        )
        weights = softmax_rows(scores)
        mixed = jnp.einsum(
            "phij,jphe->iphe", weights, value_rows, preferred_element_type=jnp.float32
        )
        return mixed.astype(jnp.bfloat16).reshape(block_rows, places, channels)

    results = lax.map(one_block, jnp.arange(blocks, dtype=jnp.int32) * block_rows)
    return results.reshape(frames, places, channels)


def squeeze_items(rows):
    return rows.reshape(rows.shape[0], rows.shape[2], rows.shape[3])


def body(
    latents,
    query_space,
    key_space,
    value_space,
    out_space,
    query_time,
    key_time,
    value_time,
    out_time,
    position_bias,
    bucket_table,
):
    frames, places, channels = latents.shape
    factor = 1.0 / math.sqrt(HEAD_DIM)
    normed = normalize(latents)
    space_q = project(normed, query_space)
    space_k = project(normed, key_space)
    space_v = project(normed, value_space)
    prior_pair = from_behind(jnp.stack([space_k[-1], space_v[-1]]), "frame", 1)
    first_pair = spread_2(jnp.stack([space_k[0], space_v[0]]), "frame", 0)
    prior_keys, prior_values = (prior_pair[0], prior_pair[1])
    first_keys, first_values = (first_pair[0], first_pair[1])
    is_first = lax.axis_index("frame") == 0
    prior_keys = jnp.where(is_first, first_keys, prior_keys)
    prior_values = jnp.where(is_first, first_values, prior_values)
    before_keys = jnp.concatenate([prior_keys[None], space_k[:-1]], axis=0)
    before_values = jnp.concatenate([prior_values[None], space_v[:-1]], axis=0)
    key_rows = jnp.concatenate([first_keys[None], before_keys], axis=1)
    value_rows = jnp.concatenate([first_values[None], before_values], axis=1)
    query_rows = space_q.reshape(frames, places, HEADS, HEAD_DIM)
    key_rows = key_rows.reshape(frames, 2 * places, HEADS, HEAD_DIM)
    value_rows = value_rows.reshape(frames, 2 * places, HEADS, HEAD_DIM)
    scores = (
        jnp.einsum("fqhe,fkhe->fhqk", query_rows, key_rows, preferred_element_type=jnp.float32)
        * factor
    )
    weights = softmax_rows(scores)
    space_mix = jnp.einsum(
        "fhqk,fkhe->fqhe", weights, value_rows, preferred_element_type=jnp.float32
    ).astype(jnp.bfloat16)
    space_out = jnp.dot(
        space_mix.reshape(-1, channels), out_space, preferred_element_type=jnp.float32
    ).reshape(frames, places, channels)
    after_space = (latents.astype(jnp.float32) + space_out).astype(jnp.bfloat16)
    normed_two = normalize(after_space)
    onehot = (
        bucket_table[:, None] == jnp.arange(position_bias.shape[1], dtype=jnp.int32)[None, :]
    ).astype(jnp.float32)
    bias_rows = jnp.dot(position_bias, onehot.T, precision=lax.Precision.HIGHEST)
    owners = lax.axis_size("frame")
    share = places // owners
    flat_rows = squeeze_items(
        lax.all_to_all(
            normed_two.reshape(frames, owners, share, channels),
            "frame",
            split_axis=1,
            concat_axis=0,
            tiled=True,
        )
    )
    mixed = temporal_attend(
        project(flat_rows, query_time),
        project(flat_rows, key_time),
        project(flat_rows, value_time),
        bias_rows,
    )
    gathered_mix = mixed[:, None]
    time_mix = lax.all_to_all(
        gathered_mix, "frame", split_axis=0, concat_axis=1, tiled=True
    ).reshape(frames, places, channels)
    time_out = jnp.dot(
        time_mix.reshape(-1, channels), out_time, preferred_element_type=jnp.float32
    ).reshape(frames, places, channels)
    return (after_space.astype(jnp.float32) + time_out).astype(jnp.bfloat16)


AXIS = "frame"
MESH = pl.DeviceIdType.MESH
LANES = 128
FAR_BELOW = -1e30
LOG2E = 1.4426950408889634


def windows(channels):
    spans = []
    for head in range(HEADS):
        begin, end = head * HEAD_DIM, (head + 1) * HEAD_DIM
        low = begin // LANES * LANES
        high = min(-(-end // LANES) * LANES, channels)
        spans.append((low, high, begin - low, end - low))
    return spans


def attend(q_ref, k_ref, v_ref, rows, scale, bias_ref):
    channels = q_ref.shape[-1]
    tiles = [None] * (channels // LANES)
    for head, (low, high, begin, end) in enumerate(windows(channels)):
        lane = lax.broadcasted_iota(jnp.int32, (rows.size, high - low), 1)
        inside = (lane >= begin) & (lane < end)
        query = q_ref[rows, low:high]
        query = jnp.where(inside, query, jnp.zeros_like(query))
        scores = lax.dot_general(
            query, k_ref[:, low:high], (((1,), (1,)), ((), ())), preferred_element_type=jnp.float32
        )
        if bias_ref is None:
            highest = jnp.max(scores, axis=-1, keepdims=True)
            powered = jnp.exp2((scores - highest) * (scale * LOG2E))
        else:
            scores = scores * scale + bias_ref[head, rows, :]
            highest = jnp.max(scores, axis=-1, keepdims=True)
            powered = jnp.exp2((scores - highest) * LOG2E)
        total = jnp.sum(powered, axis=-1, keepdims=True)
        mixed = jnp.dot(
            powered.astype(jnp.bfloat16), v_ref[:, low:high], preferred_element_type=jnp.float32
        )
        mixed = mixed * (1.0 / total)
        for at in range(low, high, LANES):
            part = mixed[:, at - low : at - low + LANES]
            keep = inside[:, at - low : at - low + LANES]
            old = tiles[at // LANES]
            tiles[at // LANES] = part if old is None else jnp.where(keep, part, old)
    return jnp.concatenate([t.astype(jnp.bfloat16) for t in tiles], axis=1)


def norm_rows(floats):
    average = jnp.mean(floats, axis=-1, keepdims=True)
    centred = floats - average
    spread = jnp.mean(centred * centred, axis=-1, keepdims=True)
    return (centred * lax.rsqrt(spread + EPS)).astype(jnp.bfloat16)


def matmul(rows, weight):
    return jnp.dot(rows, weight, preferred_element_type=jnp.float32)


def block_kernel(
    n,
    share,
    lat,
    *refs,
):
    weights, refs = refs[:8], refs[8:]
    bias_table, bucket_row, out = refs[:3]
    (
        x,
        w,
        first,
        prior,
        q,
        k,
        v,
        after,
        go,
        came,
        back_go,
        back_came,
        bias,
        pos_bias,
        buckets,
        x_sem,
        w_sem,
        t_sem,
        prior_sems,
        a_send,
        b_send,
        c_send,
        first_recv,
        go_send,
        go_recv,
        back_send,
        back_recv,
    ) = refs[3:]
    me = lax.axis_index(AXIS)
    places, channels = x.shape
    scale = 1.0 / math.sqrt(HEAD_DIM)
    other = lax.rem(me + 1, n)

    barrier = pltpu.get_barrier_semaphore()

    @pl.loop(1, n)
    def _(step):
        pl.semaphore_signal(
            barrier, inc=1, device_id={AXIS: lax.rem(me + step, n)}, device_id_type=MESH
        )

    own = pltpu.make_async_copy(lat.at[0], x, x_sem)
    own.start()
    tables = [
        pltpu.make_async_copy(bias_table, pos_bias, t_sem.at[0]),
        pltpu.make_async_copy(bucket_row, buckets, t_sem.at[1]),
    ]
    for table in tables:
        table.start()
    loads = [pltpu.make_async_copy(weights[i], w.at[i], w_sem.at[i]) for i in range(8)]
    for load in loads:
        load.start()

    pl.semaphore_wait(barrier, n - 1)

    def chunk(c):
        return lat.at[0, pl.ds(pl.multiple_of(c * share, share), share), :]

    def scatter(c):
        return pltpu.make_async_remote_copy(
            chunk(c), first.at[c], a_send.at[c], first_recv.at[c], {AXIS: c}, MESH
        )

    def gather(c, to):
        return pltpu.make_async_remote_copy(
            first.at[c], first.at[c], b_send.at[to], first_recv.at[c], {AXIS: to}, MESH
        )

    sibling = me + 1 - 2 * lax.rem(me, 2)

    def pair(c):
        return pltpu.make_async_remote_copy(
            first.at[c], first.at[c], c_send.at[c], first_recv.at[c], {AXIS: sibling}, MESH
        )

    send_prior = pltpu.make_async_remote_copy(
        lat.at[0], prior, prior_sems.at[0], prior_sems.at[1], {AXIS: other}, MESH
    )

    @pl.when(me == 0)
    def _():
        @pl.loop(1, n)
        def _(step):
            scatter(n - step).start()

    @pl.when(me < n - 1)
    def _():
        send_prior.start()

    own.wait()

    @pl.when(me == 0)
    def _():
        prior[...] = x[...]
        first[...] = x[...].reshape(n, share, channels)

    def took(c):
        pltpu.make_async_remote_copy(
            first.at[c], first.at[c], b_send.at[0], first_recv.at[c], {AXIS: other}, MESH
        ).wait_recv()

    @pl.when(me > 0)
    def _():
        took(me)

    @pl.loop(1, n // 2)
    def _(step):
        to = lax.rem(me + 2 * step, n)

        @pl.when(to != 0)
        def _():
            gather(me, to).start()

    @pl.when(sibling != 0)
    def _():
        pair(me).start()

    normed = norm_rows(x[...].astype(jnp.float32))
    loads[0].wait()
    q[...] = matmul(normed, w[0]).astype(jnp.bfloat16)

    @pl.loop(1, n // 2)
    def _(step):
        c = lax.rem(me + n - 2 * step, n)

        @pl.when(me > 0)
        def _():
            took(c)

        @pl.when(sibling != 0)
        def _():
            pair(c).start()

    @pl.when(me > 0)
    def _():
        pltpu.make_async_remote_copy(
            lat.at[0], prior, prior_sems.at[0], prior_sems.at[1], {AXIS: other}, MESH
        ).wait_recv()

    normed = norm_rows(prior[...].astype(jnp.float32))
    loads[1].wait()
    loads[2].wait()
    k[places:, :] = matmul(normed, w[1]).astype(jnp.bfloat16)
    v[places:, :] = matmul(normed, w[2]).astype(jnp.bfloat16)

    @pl.when(me > 0)
    def _():
        @pl.loop(0, n // 2)
        def _(step):
            took(2 * step + lax.rem(me + 1, 2))

    normed = norm_rows(first[...].reshape(places, channels).astype(jnp.float32))
    k[:places, :] = matmul(normed, w[1]).astype(jnp.bfloat16)
    v[:places, :] = matmul(normed, w[2]).astype(jnp.bfloat16)

    for i in range(3, 8):
        loads[i].wait()

    halves = 2
    size = places // halves

    def to_owner(to):
        return pltpu.make_async_remote_copy(
            go.at[to], came.at[me], go_send.at[to], go_recv.at[me], {AXIS: to}, MESH
        )

    def to_frame(to):
        return pltpu.make_async_remote_copy(
            back_go.at[to], back_came.at[me], back_send.at[to], back_recv.at[me], {AXIS: to}, MESH
        )

    def start_group(make, half):
        count = n // halves

        @pl.loop(0, count)
        def _(step):
            to = half * count + lax.rem(me + step, count)

            @pl.when(to != me)
            def _():
                make(to).start()

    def space_block(half):
        rows = pl.ds(pl.multiple_of(half * size, size), size)
        mix = attend(q, k, v, rows, scale, None)
        summed = x[rows, :].astype(jnp.float32) + matmul(mix, w[3])
        rounded = summed.astype(jnp.bfloat16)
        after[rows, :] = rounded
        go[pl.ds(half * (n // halves), n // halves)] = norm_rows(
            rounded.astype(jnp.float32)
        ).reshape(n // halves, share, channels)
        start_group(to_owner, half)

    pl.loop(0, halves)(space_block)

    came[pl.ds(me, 1)] = go[pl.ds(me, 1)]

    for table in tables:
        table.wait()

    onehot = (
        lax.broadcasted_iota(jnp.int32, (pos_bias.shape[1], 256), 0) == buckets[0:256].reshape(1, 256)
    ).astype(jnp.float32)
    by_offset = jnp.dot(
        pos_bias[...], onehot, precision=lax.Precision.HIGHEST, preferred_element_type=jnp.float32
    )
    limit = (buckets.shape[0] - 1) // 2
    wide = 2 * n * share
    pick = (
        lax.broadcasted_iota(jnp.int32, (256, wide), 0)
        == lax.broadcasted_iota(jnp.int32, (256, wide), 1) // share + (limit - (n - 1))
    ).astype(jnp.float32)
    spread = jnp.dot(
        by_offset, pick, precision=lax.Precision.HIGHEST, preferred_element_type=jnp.float32
    )
    same = lax.broadcasted_iota(jnp.int32, (share, n * share), 0) == lax.rem(
        lax.broadcasted_iota(jnp.int32, (share, n * share), 1), share
    )
    for i in range(n):
        begin = (n - 1 - i) * share
        line = spread[:, begin : begin + n * share]
        for head in range(HEADS):
            bias[head, i * share : (i + 1) * share, :] = jnp.where(
                same, line[head : head + 1, :], FAR_BELOW
            )

    @pl.loop(1, n)
    def _(step):
        c = lax.rem(me + step, n)
        pltpu.make_async_remote_copy(
            came.at[c], came.at[c], go_send.at[c], go_recv.at[c], {AXIS: c}, MESH
        ).wait_recv()

    rows = came[...].reshape(n * share, channels)
    q[...] = matmul(rows, w[4]).astype(jnp.bfloat16)
    k[:places, :] = matmul(rows, w[5]).astype(jnp.bfloat16)
    v[:places, :] = matmul(rows, w[6]).astype(jnp.bfloat16)

    def time_block(half):
        rows = pl.ds(pl.multiple_of(half * size, size), size)
        mix = attend(q, k.at[:places], v.at[:places], rows, scale, bias)
        back_go[pl.ds(half * (n // halves), n // halves)] = mix.reshape(
            n // halves, share, channels
        )
        start_group(to_frame, half)

    pl.loop(0, halves)(time_block)

    back_came[pl.ds(me, 1)] = back_go[pl.ds(me, 1)]

    @pl.loop(1, n)
    def _(step):
        c = lax.rem(me + step, n)
        pltpu.make_async_remote_copy(
            back_came.at[c], back_came.at[c], back_send.at[c], back_recv.at[c], {AXIS: c}, MESH
        ).wait_recv()

    mix = back_came[...].reshape(places, channels)
    out[0] = (after[...].astype(jnp.float32) + matmul(mix, w[7])).astype(jnp.bfloat16)

    @pl.when(me == 0)
    def _():
        @pl.loop(1, n)
        def _(step):
            scatter(n - step).wait_send()

    @pl.when(me < n - 1)
    def _():
        send_prior.wait_send()

    @pl.loop(1, n // 2)
    def _(step):
        to = lax.rem(me + 2 * step, n)

        @pl.when(to != 0)
        def _():
            gather(me, to).wait_send()

    @pl.when(sibling != 0)
    def _():
        @pl.loop(0, n // 2)
        def _(step):
            pair(lax.rem(me + 2 * step, n)).wait_send()

    @pl.loop(1, n)
    def _(step):
        c = lax.rem(me + step, n)
        to_owner(c).wait_send()
        to_frame(c).wait_send()


def kernel_body(
    latents,
    query_space,
    key_space,
    value_space,
    out_space,
    query_time,
    key_time,
    value_time,
    out_time,
    position_bias,
    bucket_table,
):
    _, places, channels = latents.shape
    n = lax.axis_size(AXIS)
    share = places // n
    rows = n * share
    bf16 = jnp.bfloat16
    anywhere = pl.BlockSpec(memory_space=pltpu.HBM)
    vmem = pl.BlockSpec(memory_space=pltpu.VMEM)
    blocks = pltpu.VMEM((n, share, channels), bf16)
    plane = pltpu.VMEM((places, channels), bf16)
    dma = pltpu.SemaphoreType.DMA
    return pl.pallas_call(
        functools.partial(block_kernel, n, share),
        out_shape=jax.ShapeDtypeStruct(latents.shape, bf16),
        in_specs=[anywhere] * 11,
        out_specs=vmem,
        scratch_shapes=[
            plane,
            pltpu.VMEM((8, channels, channels), bf16),
            blocks,
            plane,
            plane,
            pltpu.VMEM((2 * places, channels), bf16),
            pltpu.VMEM((2 * places, channels), bf16),
            plane,
            blocks,
            blocks,
            blocks,
            blocks,
            pltpu.VMEM((HEADS, rows, rows), jnp.float32),
            pltpu.VMEM(position_bias.shape, jnp.float32),
            pltpu.VMEM(bucket_table.shape, jnp.int32),
            dma,
            dma((8,)),
            dma((2,)),
            dma((2,)),
            dma((n,)),
            dma((n,)),
            dma((n,)),
            dma((n,)),
            dma((n,)),
            dma((n,)),
            dma((n,)),
            dma((n,)),
        ],
        compiler_params=pltpu.CompilerParams(
            collective_id=0, has_side_effects=True, vmem_limit_bytes=63 * 1024 * 1024
        ),
    )(
        latents,
        query_space,
        key_space,
        value_space,
        out_space,
        query_time,
        key_time,
        value_time,
        out_time,
        position_bias,
        bucket_table,
    )


def one_kernel(latents, *rest):
    frames, places, _ = latents.shape
    n = lax.axis_size(AXIS)
    limit = (rest[-1].shape[0] - 1) // 2
    fits = frames == 1 and n % 2 == 0 and places % (16 * n) == 0 and limit + n <= 256 and n <= limit
    return (kernel_body if fits else body)(latents, *rest)


def solution(mesh):
    in_specs = (P(("batch", "frame"), None, None), P(), P(), P(), P(), P(), P(), P(), P(), P(), P())
    out_specs = P(("batch", "frame"), None, None)
    return jax.shard_map(one_kernel, mesh=mesh, in_specs=in_specs, out_specs=out_specs, check_vma=False)
```

```python
import functools
import math

import jax
import jax.numpy as jnp
from jax import lax
from jax.experimental import pallas as pl
from jax.experimental.pallas import tpu as pltpu
from jax.sharding import PartitionSpec as P

HEADS = 8
HEAD_DIM = 80


EPS = 1e-05


def from_behind(x, axis, by):
    size = lax.axis_size(axis)
    pairs = [(i, i + by) for i in range(size) if 0 <= i + by < size]
    return lax.ppermute(x, axis, pairs)


def spread_2(block, axis, source):
    block = jnp.where(lax.axis_index(axis) == source, block, jnp.zeros_like(block))
    return lax.psum(block, axis)


def normalize(values):
    floats = values.astype(jnp.float32)
    average = jnp.mean(floats, axis=-1, keepdims=True)
    centred = floats - average
    spread = jnp.mean(centred * centred, axis=-1, keepdims=True)
    return (centred * lax.rsqrt(spread + EPS)).astype(jnp.bfloat16)


def project(rows, weight):
    lead = rows.shape[:-1]
    flat = rows.reshape(-1, rows.shape[-1])
    result = jnp.dot(flat, weight, preferred_element_type=jnp.float32)
    return result.reshape(lead + (weight.shape[1],)).astype(jnp.bfloat16)


def softmax_rows(scores):
    highest = jnp.max(scores, axis=-1, keepdims=True)
    powered = jnp.exp(scores - highest)
    return (powered / jnp.sum(powered, axis=-1, keepdims=True)).astype(jnp.bfloat16)


def temporal_attend(time_q, time_k, time_v, bias_rows):
    frames, places, channels = time_q.shape
    factor = 1.0 / math.sqrt(HEAD_DIM)
    block_rows = math.gcd(frames, 512)
    blocks = frames // block_rows
    limit = (bias_rows.shape[1] - 1) // 2
    key_rows = time_k.reshape(frames, places, HEADS, HEAD_DIM)
    value_rows = time_v.reshape(frames, places, HEADS, HEAD_DIM)
    columns = jnp.arange(frames, dtype=jnp.int32)

    def one_block(begin_row):
        query_rows = time_q.reshape(block_rows, places, HEADS, HEAD_DIM)
        row_ids = begin_row + jnp.arange(block_rows, dtype=jnp.int32)
        offsets = jnp.clip(columns[None, :] - row_ids[:, None], -limit, limit) + limit
        bias = bias_rows[:, offsets]
        scores = (
            jnp.einsum("iphe,jphe->phij", query_rows, key_rows, preferred_element_type=jnp.float32)
            * factor
            + bias[None]
        )
        weights = softmax_rows(scores)
        mixed = jnp.einsum(
            "phij,jphe->iphe", weights, value_rows, preferred_element_type=jnp.float32
        )
        return mixed.astype(jnp.bfloat16).reshape(block_rows, places, channels)

    results = lax.map(one_block, jnp.arange(blocks, dtype=jnp.int32) * block_rows)
    return results.reshape(frames, places, channels)


def squeeze_items(rows):
    return rows.reshape(rows.shape[0], rows.shape[2], rows.shape[3])


def body(
    latents,
    query_space,
    key_space,
    value_space,
    out_space,
    query_time,
    key_time,
    value_time,
    out_time,
    position_bias,
    bucket_table,
):
    frames, places, channels = latents.shape
    factor = 1.0 / math.sqrt(HEAD_DIM)
    normed = normalize(latents)
    space_q = project(normed, query_space)
    space_k = project(normed, key_space)
    space_v = project(normed, value_space)
    prior_pair = from_behind(jnp.stack([space_k[-1], space_v[-1]]), "frame", 1)
    first_pair = spread_2(jnp.stack([space_k[0], space_v[0]]), "frame", 0)
    prior_keys, prior_values = (prior_pair[0], prior_pair[1])
    first_keys, first_values = (first_pair[0], first_pair[1])
    is_first = lax.axis_index("frame") == 0
    prior_keys = jnp.where(is_first, first_keys, prior_keys)
    prior_values = jnp.where(is_first, first_values, prior_values)
    before_keys = jnp.concatenate([prior_keys[None], space_k[:-1]], axis=0)
    before_values = jnp.concatenate([prior_values[None], space_v[:-1]], axis=0)
    key_rows = jnp.concatenate([first_keys[None], before_keys], axis=1)
    value_rows = jnp.concatenate([first_values[None], before_values], axis=1)
    query_rows = space_q.reshape(frames, places, HEADS, HEAD_DIM)
    key_rows = key_rows.reshape(frames, 2 * places, HEADS, HEAD_DIM)
    value_rows = value_rows.reshape(frames, 2 * places, HEADS, HEAD_DIM)
    scores = (
        jnp.einsum("fqhe,fkhe->fhqk", query_rows, key_rows, preferred_element_type=jnp.float32)
        * factor
    )
    weights = softmax_rows(scores)
    space_mix = jnp.einsum(
        "fhqk,fkhe->fqhe", weights, value_rows, preferred_element_type=jnp.float32
    ).astype(jnp.bfloat16)
    space_out = jnp.dot(
        space_mix.reshape(-1, channels), out_space, preferred_element_type=jnp.float32
    ).reshape(frames, places, channels)
    after_space = (latents.astype(jnp.float32) + space_out).astype(jnp.bfloat16)
    normed_two = normalize(after_space)
    onehot = (
        bucket_table[:, None] == jnp.arange(position_bias.shape[1], dtype=jnp.int32)[None, :]
    ).astype(jnp.float32)
    bias_rows = jnp.dot(position_bias, onehot.T, precision=lax.Precision.HIGHEST)
    owners = lax.axis_size("frame")
    share = places // owners
    flat_rows = squeeze_items(
        lax.all_to_all(
            normed_two.reshape(frames, owners, share, channels),
            "frame",
            split_axis=1,
            concat_axis=0,
            tiled=True,
        )
    )
    mixed = temporal_attend(
        project(flat_rows, query_time),
        project(flat_rows, key_time),
        project(flat_rows, value_time),
        bias_rows,
    )
    gathered_mix = mixed[:, None]
    time_mix = lax.all_to_all(
        gathered_mix, "frame", split_axis=0, concat_axis=1, tiled=True
    ).reshape(frames, places, channels)
    time_out = jnp.dot(
        time_mix.reshape(-1, channels), out_time, preferred_element_type=jnp.float32
    ).reshape(frames, places, channels)
    return (after_space.astype(jnp.float32) + time_out).astype(jnp.bfloat16)


AXIS = "frame"
MESH = pl.DeviceIdType.MESH
LANES = 128
FAR_BELOW = -1e30
LOG2E = 1.4426950408889634


def windows(channels):
    spans = []
    for head in range(HEADS):
        begin, end = head * HEAD_DIM, (head + 1) * HEAD_DIM
        low = begin // LANES * LANES
        high = min(-(-end // LANES) * LANES, channels)
        spans.append((low, high, begin - low, end - low))
    return spans


def attend(q_ref, k_ref, v_ref, rows, scale, bias_ref):
    channels = q_ref.shape[-1]
    tiles = [None] * (channels // LANES)
    for head, (low, high, begin, end) in enumerate(windows(channels)):
        lane = lax.broadcasted_iota(jnp.int32, (rows.size, high - low), 1)
        inside = (lane >= begin) & (lane < end)
        query = q_ref[rows, low:high]
        query = jnp.where(inside, query, jnp.zeros_like(query))
        scores = lax.dot_general(
            query, k_ref[:, low:high], (((1,), (1,)), ((), ())), preferred_element_type=jnp.float32
        )
        if bias_ref is None:
            highest = jnp.max(scores, axis=-1, keepdims=True)
            powered = jnp.exp2((scores - highest) * (scale * LOG2E))
        else:
            scores = scores * scale + bias_ref[head, rows, :]
            highest = jnp.max(scores, axis=-1, keepdims=True)
            powered = jnp.exp2((scores - highest) * LOG2E)
        total = jnp.sum(powered, axis=-1, keepdims=True)
        mixed = jnp.dot(
            powered.astype(jnp.bfloat16), v_ref[:, low:high], preferred_element_type=jnp.float32
        )
        mixed = mixed * (1.0 / total)
        for at in range(low, high, LANES):
            part = mixed[:, at - low : at - low + LANES]
            keep = inside[:, at - low : at - low + LANES]
            old = tiles[at // LANES]
            tiles[at // LANES] = part if old is None else jnp.where(keep, part, old)
    return jnp.concatenate([t.astype(jnp.bfloat16) for t in tiles], axis=1)


def norm_rows(floats):
    average = jnp.mean(floats, axis=-1, keepdims=True)
    centred = floats - average
    spread = jnp.mean(centred * centred, axis=-1, keepdims=True)
    return (centred * lax.rsqrt(spread + EPS)).astype(jnp.bfloat16)


def matmul(rows, weight):
    return jnp.dot(rows, weight, preferred_element_type=jnp.float32)


def block_kernel(
    n,
    share,
    lat,
    *refs,
):
    weights, refs = refs[:8], refs[8:]
    bias_table, bucket_row, out = refs[:3]
    (
        x,
        w,
        first,
        prior,
        q,
        k,
        v,
        after,
        go,
        came,
        back_go,
        back_came,
        bias,
        pos_bias,
        buckets,
        x_sem,
        w_sem,
        t_sem,
        prior_sems,
        a_send,
        b_send,
        c_send,
        first_recv,
        go_send,
        go_recv,
        back_send,
        back_recv,
    ) = refs[3:]
    me = lax.axis_index(AXIS)
    places, channels = x.shape
    scale = 1.0 / math.sqrt(HEAD_DIM)
    other = lax.rem(me + 1, n)

    barrier = pltpu.get_barrier_semaphore()

    @pl.loop(1, n)
    def _(step):
        pl.semaphore_signal(
            barrier, inc=1, device_id={AXIS: lax.rem(me + step, n)}, device_id_type=MESH
        )

    own = pltpu.make_async_copy(lat.at[0], x, x_sem)
    own.start()
    tables = [
        pltpu.make_async_copy(bias_table, pos_bias, t_sem.at[0]),
        pltpu.make_async_copy(bucket_row, buckets, t_sem.at[1]),
    ]
    for table in tables:
        table.start()
    loads = [pltpu.make_async_copy(weights[i], w.at[i], w_sem.at[i]) for i in range(8)]
    for load in loads:
        load.start()

    pl.semaphore_wait(barrier, n - 1)

    def chunk(c):
        return lat.at[0, pl.ds(pl.multiple_of(c * share, share), share), :]

    def scatter(c):
        return pltpu.make_async_remote_copy(
            chunk(c), first.at[c], a_send.at[c], first_recv.at[c], {AXIS: c}, MESH
        )

    def gather(c, to):
        return pltpu.make_async_remote_copy(
            first.at[c], first.at[c], b_send.at[to], first_recv.at[c], {AXIS: to}, MESH
        )

    sibling = me + 1 - 2 * lax.rem(me, 2)

    def pair(c):
        return pltpu.make_async_remote_copy(
            first.at[c], first.at[c], c_send.at[c], first_recv.at[c], {AXIS: sibling}, MESH
        )

    send_prior = pltpu.make_async_remote_copy(
        lat.at[0], prior, prior_sems.at[0], prior_sems.at[1], {AXIS: other}, MESH
    )

    @pl.when(me == 0)
    def _():
        @pl.loop(1, n)
        def _(step):
            scatter(n - step).start()

    @pl.when(me < n - 1)
    def _():
        send_prior.start()

    own.wait()

    @pl.when(me == 0)
    def _():
        prior[...] = x[...]
        first[...] = x[...].reshape(n, share, channels)

    def took(c):
        pltpu.make_async_remote_copy(
            first.at[c], first.at[c], b_send.at[0], first_recv.at[c], {AXIS: other}, MESH
        ).wait_recv()

    @pl.when(me > 0)
    def _():
        took(me)

    @pl.loop(1, n // 2)
    def _(step):
        to = lax.rem(me + 2 * step, n)

        @pl.when(to != 0)
        def _():
            gather(me, to).start()

    @pl.when(sibling != 0)
    def _():
        pair(me).start()

    normed = norm_rows(x[...].astype(jnp.float32))
    loads[0].wait()
    q[...] = matmul(normed, w[0]).astype(jnp.bfloat16)

    @pl.loop(1, n // 2)
    def _(step):
        c = lax.rem(me + n - 2 * step, n)

        @pl.when(me > 0)
        def _():
            took(c)

        @pl.when(sibling != 0)
        def _():
            pair(c).start()

    @pl.when(me > 0)
    def _():
        pltpu.make_async_remote_copy(
            lat.at[0], prior, prior_sems.at[0], prior_sems.at[1], {AXIS: other}, MESH
        ).wait_recv()

    normed = norm_rows(prior[...].astype(jnp.float32))
    loads[1].wait()
    loads[2].wait()
    k[places:, :] = matmul(normed, w[1]).astype(jnp.bfloat16)
    v[places:, :] = matmul(normed, w[2]).astype(jnp.bfloat16)

    @pl.when(me > 0)
    def _():
        @pl.loop(0, n // 2)
        def _(step):
            took(2 * step + lax.rem(me + 1, 2))

    normed = norm_rows(first[...].reshape(places, channels).astype(jnp.float32))
    k[:places, :] = matmul(normed, w[1]).astype(jnp.bfloat16)
    v[:places, :] = matmul(normed, w[2]).astype(jnp.bfloat16)

    for i in range(3, 8):
        loads[i].wait()

    halves = 2
    size = places // halves

    def place(device):
        return lax.rem(device, 2) * (n // 2) + device // 2

    def to_owner(to):
        return pltpu.make_async_remote_copy(
            go.at[place(to)], came.at[me], go_send.at[to], go_recv.at[me], {AXIS: to}, MESH
        )

    def to_frame(to):
        return pltpu.make_async_remote_copy(
            back_go.at[place(to)],
            back_came.at[place(me)],
            back_send.at[to],
            back_recv.at[me],
            {AXIS: to},
            MESH,
        )

    def start_group(make, half):
        count = n // halves

        @pl.loop(0, count)
        def _(step):
            to = 2 * lax.rem(me // 2 + step, count) + half

            @pl.when(to != me)
            def _():
                make(to).start()

    def space_block(half):
        rows = pl.ds(pl.multiple_of(half * size, size), size)
        mix = attend(q, k, v, rows, scale, None)
        summed = x[rows, :].astype(jnp.float32) + matmul(mix, w[3])
        rounded = summed.astype(jnp.bfloat16)
        after[rows, :] = rounded
        go[pl.ds(half * (n // halves), n // halves)] = norm_rows(
            rounded.astype(jnp.float32)
        ).reshape(n // halves, share, channels)
        start_group(to_owner, half)

    pl.loop(0, halves)(space_block)

    came[pl.ds(me, 1)] = go[pl.ds(place(me), 1)]

    for table in tables:
        table.wait()

    onehot = (
        lax.broadcasted_iota(jnp.int32, (pos_bias.shape[1], 256), 0) == buckets[0:256].reshape(1, 256)
    ).astype(jnp.float32)
    by_offset = jnp.dot(
        pos_bias[...], onehot, precision=lax.Precision.HIGHEST, preferred_element_type=jnp.float32
    )
    limit = (buckets.shape[0] - 1) // 2
    wide = 2 * n * share
    pick = (
        lax.broadcasted_iota(jnp.int32, (256, wide), 0)
        == lax.broadcasted_iota(jnp.int32, (256, wide), 1) // share + (limit - (n - 1))
    ).astype(jnp.float32)
    spread = jnp.dot(
        by_offset, pick, precision=lax.Precision.HIGHEST, preferred_element_type=jnp.float32
    )
    same = lax.broadcasted_iota(jnp.int32, (share, n * share), 0) == lax.rem(
        lax.broadcasted_iota(jnp.int32, (share, n * share), 1), share
    )
    order = list(range(0, n, 2)) + list(range(1, n, 2))
    for block, i in enumerate(order):
        begin = (n - 1 - i) * share
        line = spread[:, begin : begin + n * share]
        for head in range(HEADS):
            bias[head, block * share : (block + 1) * share, :] = jnp.where(
                same, line[head : head + 1, :], FAR_BELOW
            )

    @pl.loop(1, n)
    def _(step):
        c = lax.rem(me + step, n)
        pltpu.make_async_remote_copy(
            came.at[c], came.at[c], go_send.at[c], go_recv.at[c], {AXIS: c}, MESH
        ).wait_recv()

    rows = came[...].reshape(n * share, channels)
    ordered = jnp.concatenate([came[i] for i in order], axis=0)
    q[...] = matmul(ordered, w[4]).astype(jnp.bfloat16)
    k[:places, :] = matmul(rows, w[5]).astype(jnp.bfloat16)
    v[:places, :] = matmul(rows, w[6]).astype(jnp.bfloat16)

    def time_block(half):
        rows = pl.ds(pl.multiple_of(half * size, size), size)
        mix = attend(q, k.at[:places], v.at[:places], rows, scale, bias)
        back_go[pl.ds(half * (n // halves), n // halves)] = mix.reshape(
            n // halves, share, channels
        )
        start_group(to_frame, half)

    pl.loop(0, halves)(time_block)

    back_came[pl.ds(place(me), 1)] = back_go[pl.ds(place(me), 1)]

    @pl.loop(1, n)
    def _(step):
        c = lax.rem(me + step, n)
        pltpu.make_async_remote_copy(
            back_came.at[place(c)],
            back_came.at[place(c)],
            back_send.at[c],
            back_recv.at[c],
            {AXIS: c},
            MESH,
        ).wait_recv()

    mix = back_came[...].reshape(places, channels)
    out[0] = (after[...].astype(jnp.float32) + matmul(mix, w[7])).astype(jnp.bfloat16)

    @pl.when(me == 0)
    def _():
        @pl.loop(1, n)
        def _(step):
            scatter(n - step).wait_send()

    @pl.when(me < n - 1)
    def _():
        send_prior.wait_send()

    @pl.loop(1, n // 2)
    def _(step):
        to = lax.rem(me + 2 * step, n)

        @pl.when(to != 0)
        def _():
            gather(me, to).wait_send()

    @pl.when(sibling != 0)
    def _():
        @pl.loop(0, n // 2)
        def _(step):
            pair(lax.rem(me + 2 * step, n)).wait_send()

    @pl.loop(1, n)
    def _(step):
        c = lax.rem(me + step, n)
        to_owner(c).wait_send()
        to_frame(c).wait_send()


def kernel_body(
    latents,
    query_space,
    key_space,
    value_space,
    out_space,
    query_time,
    key_time,
    value_time,
    out_time,
    position_bias,
    bucket_table,
):
    _, places, channels = latents.shape
    n = lax.axis_size(AXIS)
    share = places // n
    rows = n * share
    bf16 = jnp.bfloat16
    anywhere = pl.BlockSpec(memory_space=pltpu.HBM)
    vmem = pl.BlockSpec(memory_space=pltpu.VMEM)
    blocks = pltpu.VMEM((n, share, channels), bf16)
    plane = pltpu.VMEM((places, channels), bf16)
    dma = pltpu.SemaphoreType.DMA
    return pl.pallas_call(
        functools.partial(block_kernel, n, share),
        out_shape=jax.ShapeDtypeStruct(latents.shape, bf16),
        in_specs=[anywhere] * 11,
        out_specs=vmem,
        scratch_shapes=[
            plane,
            pltpu.VMEM((8, channels, channels), bf16),
            blocks,
            plane,
            plane,
            pltpu.VMEM((2 * places, channels), bf16),
            pltpu.VMEM((2 * places, channels), bf16),
            plane,
            blocks,
            blocks,
            blocks,
            blocks,
            pltpu.VMEM((HEADS, rows, rows), jnp.float32),
            pltpu.VMEM(position_bias.shape, jnp.float32),
            pltpu.VMEM(bucket_table.shape, jnp.int32),
            dma,
            dma((8,)),
            dma((2,)),
            dma((2,)),
            dma((n,)),
            dma((n,)),
            dma((n,)),
            dma((n,)),
            dma((n,)),
            dma((n,)),
            dma((n,)),
            dma((n,)),
        ],
        compiler_params=pltpu.CompilerParams(
            collective_id=0, has_side_effects=True, vmem_limit_bytes=63 * 1024 * 1024
        ),
    )(
        latents,
        query_space,
        key_space,
        value_space,
        out_space,
        query_time,
        key_time,
        value_time,
        out_time,
        position_bias,
        bucket_table,
    )


def one_kernel(latents, *rest):
    frames, places, _ = latents.shape
    n = lax.axis_size(AXIS)
    limit = (rest[-1].shape[0] - 1) // 2
    fits = frames == 1 and n % 2 == 0 and places % (16 * n) == 0 and limit + n <= 256 and n <= limit
    return (kernel_body if fits else body)(latents, *rest)


def solution(mesh):
    in_specs = (P(("batch", "frame"), None, None), P(), P(), P(), P(), P(), P(), P(), P(), P(), P())
    out_specs = P(("batch", "frame"), None, None)
    return jax.shard_map(one_kernel, mesh=mesh, in_specs=in_specs, out_specs=out_specs, check_vma=False)
```

```python
import functools
import math

import jax
import jax.numpy as jnp
from jax import lax
from jax.experimental import pallas as pl
from jax.experimental.pallas import tpu as pltpu
from jax.sharding import PartitionSpec as P

HEADS = 8
HEAD_DIM = 80


EPS = 1e-05


def from_behind(x, axis, by):
    size = lax.axis_size(axis)
    pairs = [(i, i + by) for i in range(size) if 0 <= i + by < size]
    return lax.ppermute(x, axis, pairs)


def spread_2(block, axis, source):
    block = jnp.where(lax.axis_index(axis) == source, block, jnp.zeros_like(block))
    return lax.psum(block, axis)


def normalize(values):
    floats = values.astype(jnp.float32)
    average = jnp.mean(floats, axis=-1, keepdims=True)
    centred = floats - average
    spread = jnp.mean(centred * centred, axis=-1, keepdims=True)
    return (centred * lax.rsqrt(spread + EPS)).astype(jnp.bfloat16)


def project(rows, weight):
    lead = rows.shape[:-1]
    flat = rows.reshape(-1, rows.shape[-1])
    result = jnp.dot(flat, weight, preferred_element_type=jnp.float32)
    return result.reshape(lead + (weight.shape[1],)).astype(jnp.bfloat16)


def softmax_rows(scores):
    highest = jnp.max(scores, axis=-1, keepdims=True)
    powered = jnp.exp(scores - highest)
    return (powered / jnp.sum(powered, axis=-1, keepdims=True)).astype(jnp.bfloat16)


def temporal_attend(time_q, time_k, time_v, bias_rows):
    frames, places, channels = time_q.shape
    factor = 1.0 / math.sqrt(HEAD_DIM)
    block_rows = math.gcd(frames, 512)
    blocks = frames // block_rows
    limit = (bias_rows.shape[1] - 1) // 2
    key_rows = time_k.reshape(frames, places, HEADS, HEAD_DIM)
    value_rows = time_v.reshape(frames, places, HEADS, HEAD_DIM)
    columns = jnp.arange(frames, dtype=jnp.int32)

    def one_block(begin_row):
        query_rows = time_q.reshape(block_rows, places, HEADS, HEAD_DIM)
        row_ids = begin_row + jnp.arange(block_rows, dtype=jnp.int32)
        offsets = jnp.clip(columns[None, :] - row_ids[:, None], -limit, limit) + limit
        bias = bias_rows[:, offsets]
        scores = (
            jnp.einsum("iphe,jphe->phij", query_rows, key_rows, preferred_element_type=jnp.float32)
            * factor
            + bias[None]
        )
        weights = softmax_rows(scores)
        mixed = jnp.einsum(
            "phij,jphe->iphe", weights, value_rows, preferred_element_type=jnp.float32
        )
        return mixed.astype(jnp.bfloat16).reshape(block_rows, places, channels)

    results = lax.map(one_block, jnp.arange(blocks, dtype=jnp.int32) * block_rows)
    return results.reshape(frames, places, channels)


def squeeze_items(rows):
    return rows.reshape(rows.shape[0], rows.shape[2], rows.shape[3])


def body(
    latents,
    query_space,
    key_space,
    value_space,
    out_space,
    query_time,
    key_time,
    value_time,
    out_time,
    position_bias,
    bucket_table,
):
    frames, places, channels = latents.shape
    factor = 1.0 / math.sqrt(HEAD_DIM)
    normed = normalize(latents)
    space_q = project(normed, query_space)
    space_k = project(normed, key_space)
    space_v = project(normed, value_space)
    prior_pair = from_behind(jnp.stack([space_k[-1], space_v[-1]]), "frame", 1)
    first_pair = spread_2(jnp.stack([space_k[0], space_v[0]]), "frame", 0)
    prior_keys, prior_values = (prior_pair[0], prior_pair[1])
    first_keys, first_values = (first_pair[0], first_pair[1])
    is_first = lax.axis_index("frame") == 0
    prior_keys = jnp.where(is_first, first_keys, prior_keys)
    prior_values = jnp.where(is_first, first_values, prior_values)
    before_keys = jnp.concatenate([prior_keys[None], space_k[:-1]], axis=0)
    before_values = jnp.concatenate([prior_values[None], space_v[:-1]], axis=0)
    key_rows = jnp.concatenate([first_keys[None], before_keys], axis=1)
    value_rows = jnp.concatenate([first_values[None], before_values], axis=1)
    query_rows = space_q.reshape(frames, places, HEADS, HEAD_DIM)
    key_rows = key_rows.reshape(frames, 2 * places, HEADS, HEAD_DIM)
    value_rows = value_rows.reshape(frames, 2 * places, HEADS, HEAD_DIM)
    scores = (
        jnp.einsum("fqhe,fkhe->fhqk", query_rows, key_rows, preferred_element_type=jnp.float32)
        * factor
    )
    weights = softmax_rows(scores)
    space_mix = jnp.einsum(
        "fhqk,fkhe->fqhe", weights, value_rows, preferred_element_type=jnp.float32
    ).astype(jnp.bfloat16)
    space_out = jnp.dot(
        space_mix.reshape(-1, channels), out_space, preferred_element_type=jnp.float32
    ).reshape(frames, places, channels)
    after_space = (latents.astype(jnp.float32) + space_out).astype(jnp.bfloat16)
    normed_two = normalize(after_space)
    onehot = (
        bucket_table[:, None] == jnp.arange(position_bias.shape[1], dtype=jnp.int32)[None, :]
    ).astype(jnp.float32)
    bias_rows = jnp.dot(position_bias, onehot.T, precision=lax.Precision.HIGHEST)
    owners = lax.axis_size("frame")
    share = places // owners
    flat_rows = squeeze_items(
        lax.all_to_all(
            normed_two.reshape(frames, owners, share, channels),
            "frame",
            split_axis=1,
            concat_axis=0,
            tiled=True,
        )
    )
    mixed = temporal_attend(
        project(flat_rows, query_time),
        project(flat_rows, key_time),
        project(flat_rows, value_time),
        bias_rows,
    )
    gathered_mix = mixed[:, None]
    time_mix = lax.all_to_all(
        gathered_mix, "frame", split_axis=0, concat_axis=1, tiled=True
    ).reshape(frames, places, channels)
    time_out = jnp.dot(
        time_mix.reshape(-1, channels), out_time, preferred_element_type=jnp.float32
    ).reshape(frames, places, channels)
    return (after_space.astype(jnp.float32) + time_out).astype(jnp.bfloat16)


AXIS = "frame"
MESH = pl.DeviceIdType.MESH
LANES = 128
FAR_BELOW = -1e30
LOG2E = 1.4426950408889634


def windows(channels):
    spans = []
    for head in range(HEADS):
        begin, end = head * HEAD_DIM, (head + 1) * HEAD_DIM
        low = begin // LANES * LANES
        high = min(-(-end // LANES) * LANES, channels)
        spans.append((low, high, begin - low, end - low))
    return spans


def attend(q_ref, k_ref, v_ref, rows, scale, bias_ref):
    channels = q_ref.shape[-1]
    tiles = [None] * (channels // LANES)
    for head, (low, high, begin, end) in enumerate(windows(channels)):
        lane = lax.broadcasted_iota(jnp.int32, (rows.size, high - low), 1)
        inside = (lane >= begin) & (lane < end)
        query = q_ref[rows, low:high]
        query = jnp.where(inside, query, jnp.zeros_like(query))
        scores = lax.dot_general(
            query, k_ref[:, low:high], (((1,), (1,)), ((), ())), preferred_element_type=jnp.float32
        )
        if bias_ref is None:
            highest = jnp.max(scores, axis=-1, keepdims=True)
            powered = jnp.exp2((scores - highest) * (scale * LOG2E))
        else:
            scores = scores * scale + bias_ref[head, rows, :]
            highest = jnp.max(scores, axis=-1, keepdims=True)
            powered = jnp.exp2((scores - highest) * LOG2E)
        total = jnp.sum(powered, axis=-1, keepdims=True)
        mixed = jnp.dot(
            powered.astype(jnp.bfloat16), v_ref[:, low:high], preferred_element_type=jnp.float32
        )
        mixed = mixed * (1.0 / total)
        for at in range(low, high, LANES):
            part = mixed[:, at - low : at - low + LANES]
            keep = inside[:, at - low : at - low + LANES]
            old = tiles[at // LANES]
            tiles[at // LANES] = part if old is None else jnp.where(keep, part, old)
    return jnp.concatenate([t.astype(jnp.bfloat16) for t in tiles], axis=1)


def norm_rows(floats):
    average = jnp.mean(floats, axis=-1, keepdims=True)
    centred = floats - average
    spread = jnp.mean(centred * centred, axis=-1, keepdims=True)
    return (centred * lax.rsqrt(spread + EPS)).astype(jnp.bfloat16)


def matmul(rows, weight):
    return jnp.dot(rows, weight, preferred_element_type=jnp.float32)


def block_kernel(
    n,
    share,
    lat,
    *refs,
):
    weights, refs = refs[:8], refs[8:]
    bias_table, bucket_row, out = refs[:3]
    (
        x,
        w,
        first,
        prior,
        q,
        k,
        v,
        after,
        go,
        came,
        back_go,
        back_came,
        bias,
        pos_bias,
        buckets,
        x_sem,
        w_sem,
        t_sem,
        prior_sems,
        a_send,
        b_send,
        c_send,
        first_recv,
        go_send,
        go_recv,
        back_send,
        back_recv,
    ) = refs[3:]
    me = lax.axis_index(AXIS)
    places, channels = x.shape
    scale = 1.0 / math.sqrt(HEAD_DIM)
    other = lax.rem(me + 1, n)

    barrier = pltpu.get_barrier_semaphore()

    @pl.loop(1, n)
    def _(step):
        pl.semaphore_signal(
            barrier, inc=1, device_id={AXIS: lax.rem(me + step, n)}, device_id_type=MESH
        )

    own = pltpu.make_async_copy(lat.at[0], x, x_sem)
    own.start()
    tables = [
        pltpu.make_async_copy(bias_table, pos_bias, t_sem.at[0]),
        pltpu.make_async_copy(bucket_row, buckets, t_sem.at[1]),
    ]
    for table in tables:
        table.start()
    loads = [pltpu.make_async_copy(weights[i], w.at[i], w_sem.at[i]) for i in range(8)]
    for load in loads:
        load.start()

    pl.semaphore_wait(barrier, n - 1)

    def chunk(c):
        return lat.at[0, pl.ds(pl.multiple_of(c * share, share), share), :]

    def scatter(c):
        return pltpu.make_async_remote_copy(
            chunk(c), first.at[c], a_send.at[c], first_recv.at[c], {AXIS: c}, MESH
        )

    def gather(c, to):
        return pltpu.make_async_remote_copy(
            first.at[c], first.at[c], b_send.at[to], first_recv.at[c], {AXIS: to}, MESH
        )

    sibling = me + 1 - 2 * lax.rem(me, 2)

    def pair(c):
        return pltpu.make_async_remote_copy(
            first.at[c], first.at[c], c_send.at[c], first_recv.at[c], {AXIS: sibling}, MESH
        )

    send_prior = pltpu.make_async_remote_copy(
        lat.at[0], prior, prior_sems.at[0], prior_sems.at[1], {AXIS: other}, MESH
    )

    @pl.when(me == 0)
    def _():
        @pl.loop(1, n)
        def _(step):
            scatter(n - step).start()

    @pl.when(me < n - 1)
    def _():
        send_prior.start()

    own.wait()

    @pl.when(me == 0)
    def _():
        prior[...] = x[...]
        first[...] = x[...].reshape(n, share, channels)

    def took(c):
        pltpu.make_async_remote_copy(
            first.at[c], first.at[c], b_send.at[0], first_recv.at[c], {AXIS: other}, MESH
        ).wait_recv()

    @pl.when(me > 0)
    def _():
        took(me)

    @pl.loop(1, n // 2)
    def _(step):
        to = lax.rem(me + 2 * step, n)

        @pl.when(to != 0)
        def _():
            gather(me, to).start()

    @pl.when(sibling != 0)
    def _():
        pair(me).start()

    normed = norm_rows(x[...].astype(jnp.float32))
    loads[0].wait()
    q[...] = matmul(normed, w[0]).astype(jnp.bfloat16)

    @pl.loop(1, n // 2)
    def _(step):
        c = lax.rem(me + n - 2 * step, n)

        @pl.when(me > 0)
        def _():
            took(c)

        @pl.when(sibling != 0)
        def _():
            pair(c).start()

    @pl.when(me > 0)
    def _():
        pltpu.make_async_remote_copy(
            lat.at[0], prior, prior_sems.at[0], prior_sems.at[1], {AXIS: other}, MESH
        ).wait_recv()

    normed = norm_rows(prior[...].astype(jnp.float32))
    loads[1].wait()
    loads[2].wait()
    k[places:, :] = matmul(normed, w[1]).astype(jnp.bfloat16)
    v[places:, :] = matmul(normed, w[2]).astype(jnp.bfloat16)

    @pl.when(me > 0)
    def _():
        @pl.loop(0, n // 2)
        def _(step):
            took(2 * step + lax.rem(me + 1, 2))

    normed = norm_rows(first[...].reshape(places, channels).astype(jnp.float32))
    k[:places, :] = matmul(normed, w[1]).astype(jnp.bfloat16)
    v[:places, :] = matmul(normed, w[2]).astype(jnp.bfloat16)

    for i in range(3, 8):
        loads[i].wait()

    halves = 4
    size = places // halves

    def place(device):
        return lax.rem(device + device // 4, 4) * (n // 4) + device // 4

    def to_owner(to):
        return pltpu.make_async_remote_copy(
            go.at[place(to)], came.at[me], go_send.at[to], go_recv.at[me], {AXIS: to}, MESH
        )

    def to_frame(to):
        return pltpu.make_async_remote_copy(
            back_go.at[place(to)],
            back_came.at[place(me)],
            back_send.at[to],
            back_recv.at[me],
            {AXIS: to},
            MESH,
        )

    def start_group(make, half):
        count = n // halves

        @pl.loop(0, count)
        def _(step):
            far = lax.rem(me // 4 + step, count)
            to = 4 * far + lax.rem(half + 3 * far, 4)

            @pl.when(to != me)
            def _():
                make(to).start()

    def space_block(half):
        rows = pl.ds(pl.multiple_of(half * size, size), size)
        mix = attend(q, k, v, rows, scale, None)
        summed = x[rows, :].astype(jnp.float32) + matmul(mix, w[3])
        rounded = summed.astype(jnp.bfloat16)
        after[rows, :] = rounded
        go[pl.ds(half * (n // halves), n // halves)] = norm_rows(
            rounded.astype(jnp.float32)
        ).reshape(n // halves, share, channels)
        start_group(to_owner, half)

    pl.loop(0, halves)(space_block)

    came[pl.ds(me, 1)] = go[pl.ds(place(me), 1)]

    for table in tables:
        table.wait()

    onehot = (
        lax.broadcasted_iota(jnp.int32, (pos_bias.shape[1], 256), 0) == buckets[0:256].reshape(1, 256)
    ).astype(jnp.float32)
    by_offset = jnp.dot(
        pos_bias[...], onehot, precision=lax.Precision.HIGHEST, preferred_element_type=jnp.float32
    )
    limit = (buckets.shape[0] - 1) // 2
    wide = 2 * n * share
    pick = (
        lax.broadcasted_iota(jnp.int32, (256, wide), 0)
        == lax.broadcasted_iota(jnp.int32, (256, wide), 1) // share + (limit - (n - 1))
    ).astype(jnp.float32)
    spread = jnp.dot(
        by_offset, pick, precision=lax.Precision.HIGHEST, preferred_element_type=jnp.float32
    )
    same = lax.broadcasted_iota(jnp.int32, (share, n * share), 0) == lax.rem(
        lax.broadcasted_iota(jnp.int32, (share, n * share), 1), share
    )
    order = [4 * far + (group - far) % 4 for group in range(4) for far in range(n // 4)]
    for block, i in enumerate(order):
        begin = (n - 1 - i) * share
        line = spread[:, begin : begin + n * share]
        for head in range(HEADS):
            bias[head, block * share : (block + 1) * share, :] = jnp.where(
                same, line[head : head + 1, :], FAR_BELOW
            )

    @pl.loop(1, n)
    def _(step):
        c = lax.rem(me + step, n)
        pltpu.make_async_remote_copy(
            came.at[c], came.at[c], go_send.at[c], go_recv.at[c], {AXIS: c}, MESH
        ).wait_recv()

    rows = came[...].reshape(n * share, channels)
    ordered = jnp.concatenate([came[i] for i in order], axis=0)
    q[...] = matmul(ordered, w[4]).astype(jnp.bfloat16)
    k[:places, :] = matmul(rows, w[5]).astype(jnp.bfloat16)
    v[:places, :] = matmul(rows, w[6]).astype(jnp.bfloat16)

    def time_block(half):
        rows = pl.ds(pl.multiple_of(half * size, size), size)
        mix = attend(q, k.at[:places], v.at[:places], rows, scale, bias)
        back_go[pl.ds(half * (n // halves), n // halves)] = mix.reshape(
            n // halves, share, channels
        )
        start_group(to_frame, half)

    pl.loop(0, halves)(time_block)

    back_came[pl.ds(place(me), 1)] = back_go[pl.ds(place(me), 1)]

    @pl.loop(1, n)
    def _(step):
        c = lax.rem(me + step, n)
        pltpu.make_async_remote_copy(
            back_came.at[place(c)],
            back_came.at[place(c)],
            back_send.at[c],
            back_recv.at[c],
            {AXIS: c},
            MESH,
        ).wait_recv()

    mix = back_came[...].reshape(places, channels)
    out[0] = (after[...].astype(jnp.float32) + matmul(mix, w[7])).astype(jnp.bfloat16)

    @pl.when(me == 0)
    def _():
        @pl.loop(1, n)
        def _(step):
            scatter(n - step).wait_send()

    @pl.when(me < n - 1)
    def _():
        send_prior.wait_send()

    @pl.loop(1, n // 2)
    def _(step):
        to = lax.rem(me + 2 * step, n)

        @pl.when(to != 0)
        def _():
            gather(me, to).wait_send()

    @pl.when(sibling != 0)
    def _():
        @pl.loop(0, n // 2)
        def _(step):
            pair(lax.rem(me + 2 * step, n)).wait_send()

    @pl.loop(1, n)
    def _(step):
        c = lax.rem(me + step, n)
        to_owner(c).wait_send()
        to_frame(c).wait_send()


def kernel_body(
    latents,
    query_space,
    key_space,
    value_space,
    out_space,
    query_time,
    key_time,
    value_time,
    out_time,
    position_bias,
    bucket_table,
):
    _, places, channels = latents.shape
    n = lax.axis_size(AXIS)
    share = places // n
    rows = n * share
    bf16 = jnp.bfloat16
    anywhere = pl.BlockSpec(memory_space=pltpu.HBM)
    vmem = pl.BlockSpec(memory_space=pltpu.VMEM)
    blocks = pltpu.VMEM((n, share, channels), bf16)
    plane = pltpu.VMEM((places, channels), bf16)
    dma = pltpu.SemaphoreType.DMA
    return pl.pallas_call(
        functools.partial(block_kernel, n, share),
        out_shape=jax.ShapeDtypeStruct(latents.shape, bf16),
        in_specs=[anywhere] * 11,
        out_specs=vmem,
        scratch_shapes=[
            plane,
            pltpu.VMEM((8, channels, channels), bf16),
            blocks,
            plane,
            plane,
            pltpu.VMEM((2 * places, channels), bf16),
            pltpu.VMEM((2 * places, channels), bf16),
            plane,
            blocks,
            blocks,
            blocks,
            blocks,
            pltpu.VMEM((HEADS, rows, rows), jnp.float32),
            pltpu.VMEM(position_bias.shape, jnp.float32),
            pltpu.VMEM(bucket_table.shape, jnp.int32),
            dma,
            dma((8,)),
            dma((2,)),
            dma((2,)),
            dma((n,)),
            dma((n,)),
            dma((n,)),
            dma((n,)),
            dma((n,)),
            dma((n,)),
            dma((n,)),
            dma((n,)),
        ],
        compiler_params=pltpu.CompilerParams(
            collective_id=0, has_side_effects=True, vmem_limit_bytes=63 * 1024 * 1024
        ),
    )(
        latents,
        query_space,
        key_space,
        value_space,
        out_space,
        query_time,
        key_time,
        value_time,
        out_time,
        position_bias,
        bucket_table,
    )


def one_kernel(latents, *rest):
    frames, places, _ = latents.shape
    n = lax.axis_size(AXIS)
    limit = (rest[-1].shape[0] - 1) // 2
    fits = frames == 1 and n % 4 == 0 and places % (16 * n) == 0 and limit + n <= 256 and n <= limit
    return (kernel_body if fits else body)(latents, *rest)


def solution(mesh):
    in_specs = (P(("batch", "frame"), None, None), P(), P(), P(), P(), P(), P(), P(), P(), P(), P())
    out_specs = P(("batch", "frame"), None, None)
    return jax.shard_map(one_kernel, mesh=mesh, in_specs=in_specs, out_specs=out_specs, check_vma=False)
```

```python
import functools
import math

import jax
import jax.numpy as jnp
from jax import lax
from jax.experimental import pallas as pl
from jax.experimental.pallas import tpu as pltpu
from jax.sharding import PartitionSpec as P

HEADS = 8
HEAD_DIM = 80


EPS = 1e-05


def from_behind(x, axis, by):
    size = lax.axis_size(axis)
    pairs = [(i, i + by) for i in range(size) if 0 <= i + by < size]
    return lax.ppermute(x, axis, pairs)


def spread_2(block, axis, source):
    block = jnp.where(lax.axis_index(axis) == source, block, jnp.zeros_like(block))
    return lax.psum(block, axis)


def normalize(values):
    floats = values.astype(jnp.float32)
    average = jnp.mean(floats, axis=-1, keepdims=True)
    centred = floats - average
    spread = jnp.mean(centred * centred, axis=-1, keepdims=True)
    return (centred * lax.rsqrt(spread + EPS)).astype(jnp.bfloat16)


def project(rows, weight):
    lead = rows.shape[:-1]
    flat = rows.reshape(-1, rows.shape[-1])
    result = jnp.dot(flat, weight, preferred_element_type=jnp.float32)
    return result.reshape(lead + (weight.shape[1],)).astype(jnp.bfloat16)


def softmax_rows(scores):
    highest = jnp.max(scores, axis=-1, keepdims=True)
    powered = jnp.exp(scores - highest)
    return (powered / jnp.sum(powered, axis=-1, keepdims=True)).astype(jnp.bfloat16)


def temporal_attend(time_q, time_k, time_v, bias_rows):
    frames, places, channels = time_q.shape
    factor = 1.0 / math.sqrt(HEAD_DIM)
    block_rows = math.gcd(frames, 512)
    blocks = frames // block_rows
    limit = (bias_rows.shape[1] - 1) // 2
    key_rows = time_k.reshape(frames, places, HEADS, HEAD_DIM)
    value_rows = time_v.reshape(frames, places, HEADS, HEAD_DIM)
    columns = jnp.arange(frames, dtype=jnp.int32)

    def one_block(begin_row):
        query_rows = time_q.reshape(block_rows, places, HEADS, HEAD_DIM)
        row_ids = begin_row + jnp.arange(block_rows, dtype=jnp.int32)
        offsets = jnp.clip(columns[None, :] - row_ids[:, None], -limit, limit) + limit
        bias = bias_rows[:, offsets]
        scores = (
            jnp.einsum("iphe,jphe->phij", query_rows, key_rows, preferred_element_type=jnp.float32)
            * factor
            + bias[None]
        )
        weights = softmax_rows(scores)
        mixed = jnp.einsum(
            "phij,jphe->iphe", weights, value_rows, preferred_element_type=jnp.float32
        )
        return mixed.astype(jnp.bfloat16).reshape(block_rows, places, channels)

    results = lax.map(one_block, jnp.arange(blocks, dtype=jnp.int32) * block_rows)
    return results.reshape(frames, places, channels)


def squeeze_items(rows):
    return rows.reshape(rows.shape[0], rows.shape[2], rows.shape[3])


def body(
    latents,
    query_space,
    key_space,
    value_space,
    out_space,
    query_time,
    key_time,
    value_time,
    out_time,
    position_bias,
    bucket_table,
):
    frames, places, channels = latents.shape
    factor = 1.0 / math.sqrt(HEAD_DIM)
    normed = normalize(latents)
    space_q = project(normed, query_space)
    space_k = project(normed, key_space)
    space_v = project(normed, value_space)
    prior_pair = from_behind(jnp.stack([space_k[-1], space_v[-1]]), "frame", 1)
    first_pair = spread_2(jnp.stack([space_k[0], space_v[0]]), "frame", 0)
    prior_keys, prior_values = (prior_pair[0], prior_pair[1])
    first_keys, first_values = (first_pair[0], first_pair[1])
    is_first = lax.axis_index("frame") == 0
    prior_keys = jnp.where(is_first, first_keys, prior_keys)
    prior_values = jnp.where(is_first, first_values, prior_values)
    before_keys = jnp.concatenate([prior_keys[None], space_k[:-1]], axis=0)
    before_values = jnp.concatenate([prior_values[None], space_v[:-1]], axis=0)
    key_rows = jnp.concatenate([first_keys[None], before_keys], axis=1)
    value_rows = jnp.concatenate([first_values[None], before_values], axis=1)
    query_rows = space_q.reshape(frames, places, HEADS, HEAD_DIM)
    key_rows = key_rows.reshape(frames, 2 * places, HEADS, HEAD_DIM)
    value_rows = value_rows.reshape(frames, 2 * places, HEADS, HEAD_DIM)
    scores = (
        jnp.einsum("fqhe,fkhe->fhqk", query_rows, key_rows, preferred_element_type=jnp.float32)
        * factor
    )
    weights = softmax_rows(scores)
    space_mix = jnp.einsum(
        "fhqk,fkhe->fqhe", weights, value_rows, preferred_element_type=jnp.float32
    ).astype(jnp.bfloat16)
    space_out = jnp.dot(
        space_mix.reshape(-1, channels), out_space, preferred_element_type=jnp.float32
    ).reshape(frames, places, channels)
    after_space = (latents.astype(jnp.float32) + space_out).astype(jnp.bfloat16)
    normed_two = normalize(after_space)
    onehot = (
        bucket_table[:, None] == jnp.arange(position_bias.shape[1], dtype=jnp.int32)[None, :]
    ).astype(jnp.float32)
    bias_rows = jnp.dot(position_bias, onehot.T, precision=lax.Precision.HIGHEST)
    owners = lax.axis_size("frame")
    share = places // owners
    flat_rows = squeeze_items(
        lax.all_to_all(
            normed_two.reshape(frames, owners, share, channels),
            "frame",
            split_axis=1,
            concat_axis=0,
            tiled=True,
        )
    )
    mixed = temporal_attend(
        project(flat_rows, query_time),
        project(flat_rows, key_time),
        project(flat_rows, value_time),
        bias_rows,
    )
    gathered_mix = mixed[:, None]
    time_mix = lax.all_to_all(
        gathered_mix, "frame", split_axis=0, concat_axis=1, tiled=True
    ).reshape(frames, places, channels)
    time_out = jnp.dot(
        time_mix.reshape(-1, channels), out_time, preferred_element_type=jnp.float32
    ).reshape(frames, places, channels)
    return (after_space.astype(jnp.float32) + time_out).astype(jnp.bfloat16)


AXIS = "frame"
MESH = pl.DeviceIdType.MESH
LANES = 128
FAR_BELOW = -1e30
LOG2E = 1.4426950408889634


def windows(channels):
    spans = []
    for head in range(HEADS):
        begin, end = head * HEAD_DIM, (head + 1) * HEAD_DIM
        low = begin // LANES * LANES
        high = min(-(-end // LANES) * LANES, channels)
        spans.append((low, high, begin - low, end - low))
    return spans


def attend(q_ref, k_ref, v_ref, rows, scale, bias_ref, acc=None, stat=None):
    channels = q_ref.shape[-1]
    tiles = [None] * (channels // LANES)
    for head, (low, high, begin, end) in enumerate(windows(channels)):
        lane = lax.broadcasted_iota(jnp.int32, (rows.size, high - low), 1)
        inside = (lane >= begin) & (lane < end)
        query = q_ref[rows, low:high]
        query = jnp.where(inside, query, jnp.zeros_like(query))
        scores = lax.dot_general(
            query, k_ref[:, low:high], (((1,), (1,)), ((), ())), preferred_element_type=jnp.float32
        )
        if bias_ref is None:
            before = stat[head, rows, 0:1]
            highest = jnp.maximum(jnp.max(scores, axis=-1, keepdims=True), before)
            powered = jnp.exp2((scores - highest) * (scale * LOG2E))
        else:
            scores = scores * scale + bias_ref[head, rows, :]
            highest = jnp.max(scores, axis=-1, keepdims=True)
            powered = jnp.exp2((scores - highest) * LOG2E)
        total = jnp.sum(powered, axis=-1, keepdims=True)
        mixed = jnp.dot(
            powered.astype(jnp.bfloat16), v_ref[:, low:high], preferred_element_type=jnp.float32
        )
        if bias_ref is None:
            fade = jnp.exp2((before - highest) * (scale * LOG2E))
            total = total + stat[head, rows, 1:2] * fade
            mixed = mixed + acc[head, rows, : high - low] * fade
        mixed = mixed * (1.0 / total)
        for at in range(low, high, LANES):
            part = mixed[:, at - low : at - low + LANES]
            keep = inside[:, at - low : at - low + LANES]
            old = tiles[at // LANES]
            tiles[at // LANES] = part if old is None else jnp.where(keep, part, old)
    return jnp.concatenate([t.astype(jnp.bfloat16) for t in tiles], axis=1)


def attend_prior(q_ref, k_ref, v_ref, rows, scale, acc, stat):
    for head, (low, high, begin, end) in enumerate(windows(q_ref.shape[-1])):
        lane = lax.broadcasted_iota(jnp.int32, (rows.size, high - low), 1)
        query = q_ref[rows, low:high]
        query = jnp.where((lane >= begin) & (lane < end), query, jnp.zeros_like(query))
        scores = lax.dot_general(
            query, k_ref[:, low:high], (((1,), (1,)), ((), ())), preferred_element_type=jnp.float32
        )
        highest = jnp.max(scores, axis=-1, keepdims=True)
        powered = jnp.exp2((scores - highest) * (scale * LOG2E))
        stat[head, rows, 0:1] = highest
        stat[head, rows, 1:2] = jnp.sum(powered, axis=-1, keepdims=True)
        acc[head, rows, : high - low] = jnp.dot(
            powered.astype(jnp.bfloat16), v_ref[:, low:high], preferred_element_type=jnp.float32
        )


def norm_rows(floats):
    average = jnp.mean(floats, axis=-1, keepdims=True)
    centred = floats - average
    spread = jnp.mean(centred * centred, axis=-1, keepdims=True)
    return (centred * lax.rsqrt(spread + EPS)).astype(jnp.bfloat16)


def matmul(rows, weight):
    return jnp.dot(rows, weight, preferred_element_type=jnp.float32)


def block_kernel(
    n,
    share,
    lat,
    *refs,
):
    weights, refs = refs[:8], refs[8:]
    bias_table, bucket_row, out = refs[:3]
    (
        x,
        w,
        first,
        prior,
        q,
        k,
        v,
        after,
        go,
        came,
        back_go,
        back_came,
        bias,
        acc,
        stat,
        pos_bias,
        buckets,
        x_sem,
        w_sem,
        t_sem,
        prior_sems,
        a_send,
        b_send,
        c_send,
        first_recv,
        go_send,
        go_recv,
        back_send,
        back_recv,
    ) = refs[3:]
    me = lax.axis_index(AXIS)
    places, channels = x.shape
    scale = 1.0 / math.sqrt(HEAD_DIM)
    other = lax.rem(me + 1, n)

    barrier = pltpu.get_barrier_semaphore()

    @pl.loop(1, n)
    def _(step):
        pl.semaphore_signal(
            barrier, inc=1, device_id={AXIS: lax.rem(me + step, n)}, device_id_type=MESH
        )

    own = pltpu.make_async_copy(lat.at[0], x, x_sem)
    own.start()
    tables = [
        pltpu.make_async_copy(bias_table, pos_bias, t_sem.at[0]),
        pltpu.make_async_copy(bucket_row, buckets, t_sem.at[1]),
    ]
    for table in tables:
        table.start()
    loads = [pltpu.make_async_copy(weights[i], w.at[i], w_sem.at[i]) for i in range(8)]
    for load in loads:
        load.start()

    pl.semaphore_wait(barrier, n - 1)

    def chunk(c):
        return lat.at[0, pl.ds(pl.multiple_of(c * share, share), share), :]

    def scatter(c):
        return pltpu.make_async_remote_copy(
            chunk(c), first.at[c], a_send.at[c], first_recv.at[c], {AXIS: c}, MESH
        )

    def gather(c, to):
        return pltpu.make_async_remote_copy(
            first.at[c], first.at[c], b_send.at[to], first_recv.at[c], {AXIS: to}, MESH
        )

    sibling = me + 1 - 2 * lax.rem(me, 2)

    def pair(c):
        return pltpu.make_async_remote_copy(
            first.at[c], first.at[c], c_send.at[c], first_recv.at[c], {AXIS: sibling}, MESH
        )

    send_prior = pltpu.make_async_remote_copy(
        lat.at[0], prior, prior_sems.at[0], prior_sems.at[1], {AXIS: other}, MESH
    )

    @pl.when(me == 0)
    def _():
        @pl.loop(1, n)
        def _(step):
            scatter(n - step).start()

    @pl.when(me < n - 1)
    def _():
        send_prior.start()

    own.wait()

    @pl.when(me == 0)
    def _():
        prior[...] = x[...]
        first[...] = x[...].reshape(n, share, channels)

    def took(c):
        pltpu.make_async_remote_copy(
            first.at[c], first.at[c], b_send.at[0], first_recv.at[c], {AXIS: other}, MESH
        ).wait_recv()

    @pl.when(me > 0)
    def _():
        took(me)

    @pl.loop(1, n // 2)
    def _(step):
        to = lax.rem(me + 2 * step, n)

        @pl.when(to != 0)
        def _():
            gather(me, to).start()

    @pl.when(sibling != 0)
    def _():
        pair(me).start()

    normed = norm_rows(x[...].astype(jnp.float32))
    loads[0].wait()
    q[...] = matmul(normed, w[0]).astype(jnp.bfloat16)

    @pl.loop(1, n // 2)
    def _(step):
        c = lax.rem(me + n - 2 * step, n)

        @pl.when(me > 0)
        def _():
            took(c)

        @pl.when(sibling != 0)
        def _():
            pair(c).start()

    @pl.when(me > 0)
    def _():
        pltpu.make_async_remote_copy(
            lat.at[0], prior, prior_sems.at[0], prior_sems.at[1], {AXIS: other}, MESH
        ).wait_recv()

    normed = norm_rows(prior[...].astype(jnp.float32))
    loads[1].wait()
    loads[2].wait()
    k[places:, :] = matmul(normed, w[1]).astype(jnp.bfloat16)
    v[places:, :] = matmul(normed, w[2]).astype(jnp.bfloat16)

    halves = 2
    size = places // halves

    def prior_block(half):
        rows = pl.ds(pl.multiple_of(half * size, size), size)
        attend_prior(q, k.at[places:], v.at[places:], rows, scale, acc, stat)

    pl.loop(0, halves)(prior_block)

    @pl.when(me > 0)
    def _():
        @pl.loop(0, n // 2)
        def _(step):
            took(2 * step + lax.rem(me + 1, 2))

    normed = norm_rows(first[...].reshape(places, channels).astype(jnp.float32))
    k[:places, :] = matmul(normed, w[1]).astype(jnp.bfloat16)
    v[:places, :] = matmul(normed, w[2]).astype(jnp.bfloat16)

    for i in range(3, 8):
        loads[i].wait()

    def place(device):
        return lax.rem(device, 2) * (n // 2) + device // 2

    def to_owner(to):
        return pltpu.make_async_remote_copy(
            go.at[place(to)], came.at[me], go_send.at[to], go_recv.at[me], {AXIS: to}, MESH
        )

    def to_frame(to):
        return pltpu.make_async_remote_copy(
            back_go.at[place(to)],
            back_came.at[place(me)],
            back_send.at[to],
            back_recv.at[me],
            {AXIS: to},
            MESH,
        )

    def start_group(make, half):
        count = n // halves

        @pl.loop(0, count)
        def _(step):
            to = 2 * lax.rem(me // 2 + step, count) + half

            @pl.when(to != me)
            def _():
                make(to).start()

    def space_block(half):
        rows = pl.ds(pl.multiple_of(half * size, size), size)
        mix = attend(q, k.at[:places], v.at[:places], rows, scale, None, acc, stat)
        summed = x[rows, :].astype(jnp.float32) + matmul(mix, w[3])
        rounded = summed.astype(jnp.bfloat16)
        after[rows, :] = rounded
        go[pl.ds(half * (n // halves), n // halves)] = norm_rows(
            rounded.astype(jnp.float32)
        ).reshape(n // halves, share, channels)
        start_group(to_owner, half)

    pl.loop(0, halves)(space_block)

    came[pl.ds(me, 1)] = go[pl.ds(place(me), 1)]

    for table in tables:
        table.wait()

    onehot = (
        lax.broadcasted_iota(jnp.int32, (pos_bias.shape[1], 256), 0) == buckets[0:256].reshape(1, 256)
    ).astype(jnp.float32)
    by_offset = jnp.dot(
        pos_bias[...], onehot, precision=lax.Precision.HIGHEST, preferred_element_type=jnp.float32
    )
    limit = (buckets.shape[0] - 1) // 2
    wide = 2 * n * share
    pick = (
        lax.broadcasted_iota(jnp.int32, (256, wide), 0)
        == lax.broadcasted_iota(jnp.int32, (256, wide), 1) // share + (limit - (n - 1))
    ).astype(jnp.float32)
    spread = jnp.dot(
        by_offset, pick, precision=lax.Precision.HIGHEST, preferred_element_type=jnp.float32
    )
    same = lax.broadcasted_iota(jnp.int32, (share, n * share), 0) == lax.rem(
        lax.broadcasted_iota(jnp.int32, (share, n * share), 1), share
    )
    order = list(range(0, n, 2)) + list(range(1, n, 2))
    for block, i in enumerate(order):
        begin = (n - 1 - i) * share
        line = spread[:, begin : begin + n * share]
        for head in range(HEADS):
            bias[head, block * share : (block + 1) * share, :] = jnp.where(
                same, line[head : head + 1, :], FAR_BELOW
            )

    @pl.loop(1, n)
    def _(step):
        c = lax.rem(me + step, n)
        pltpu.make_async_remote_copy(
            came.at[c], came.at[c], go_send.at[c], go_recv.at[c], {AXIS: c}, MESH
        ).wait_recv()

    rows = came[...].reshape(n * share, channels)
    ordered = jnp.concatenate([came[i] for i in order], axis=0)
    q[...] = matmul(ordered, w[4]).astype(jnp.bfloat16)
    k[:places, :] = matmul(rows, w[5]).astype(jnp.bfloat16)
    v[:places, :] = matmul(rows, w[6]).astype(jnp.bfloat16)

    def time_block(half):
        rows = pl.ds(pl.multiple_of(half * size, size), size)
        mix = attend(q, k.at[:places], v.at[:places], rows, scale, bias)
        back_go[pl.ds(half * (n // halves), n // halves)] = mix.reshape(
            n // halves, share, channels
        )
        start_group(to_frame, half)

    pl.loop(0, halves)(time_block)

    back_came[pl.ds(place(me), 1)] = back_go[pl.ds(place(me), 1)]

    @pl.loop(1, n)
    def _(step):
        c = lax.rem(me + step, n)
        pltpu.make_async_remote_copy(
            back_came.at[place(c)],
            back_came.at[place(c)],
            back_send.at[c],
            back_recv.at[c],
            {AXIS: c},
            MESH,
        ).wait_recv()

    mix = back_came[...].reshape(places, channels)
    out[0] = (after[...].astype(jnp.float32) + matmul(mix, w[7])).astype(jnp.bfloat16)

    @pl.when(me == 0)
    def _():
        @pl.loop(1, n)
        def _(step):
            scatter(n - step).wait_send()

    @pl.when(me < n - 1)
    def _():
        send_prior.wait_send()

    @pl.loop(1, n // 2)
    def _(step):
        to = lax.rem(me + 2 * step, n)

        @pl.when(to != 0)
        def _():
            gather(me, to).wait_send()

    @pl.when(sibling != 0)
    def _():
        @pl.loop(0, n // 2)
        def _(step):
            pair(lax.rem(me + 2 * step, n)).wait_send()

    @pl.loop(1, n)
    def _(step):
        c = lax.rem(me + step, n)
        to_owner(c).wait_send()
        to_frame(c).wait_send()


def kernel_body(
    latents,
    query_space,
    key_space,
    value_space,
    out_space,
    query_time,
    key_time,
    value_time,
    out_time,
    position_bias,
    bucket_table,
):
    _, places, channels = latents.shape
    n = lax.axis_size(AXIS)
    share = places // n
    rows = n * share
    bf16 = jnp.bfloat16
    anywhere = pl.BlockSpec(memory_space=pltpu.HBM)
    vmem = pl.BlockSpec(memory_space=pltpu.VMEM)
    blocks = pltpu.VMEM((n, share, channels), bf16)
    plane = pltpu.VMEM((places, channels), bf16)
    dma = pltpu.SemaphoreType.DMA
    return pl.pallas_call(
        functools.partial(block_kernel, n, share),
        out_shape=jax.ShapeDtypeStruct(latents.shape, bf16),
        in_specs=[anywhere] * 11,
        out_specs=vmem,
        scratch_shapes=[
            plane,
            pltpu.VMEM((8, channels, channels), bf16),
            blocks,
            plane,
            plane,
            pltpu.VMEM((2 * places, channels), bf16),
            pltpu.VMEM((2 * places, channels), bf16),
            plane,
            blocks,
            blocks,
            blocks,
            blocks,
            pltpu.VMEM((HEADS, rows, rows), jnp.float32),
            pltpu.VMEM((HEADS, places, 2 * LANES), jnp.float32),
            pltpu.VMEM((HEADS, places, LANES), jnp.float32),
            pltpu.VMEM(position_bias.shape, jnp.float32),
            pltpu.VMEM(bucket_table.shape, jnp.int32),
            dma,
            dma((8,)),
            dma((2,)),
            dma((2,)),
            dma((n,)),
            dma((n,)),
            dma((n,)),
            dma((n,)),
            dma((n,)),
            dma((n,)),
            dma((n,)),
            dma((n,)),
        ],
        compiler_params=pltpu.CompilerParams(
            collective_id=0, has_side_effects=True, vmem_limit_bytes=63 * 1024 * 1024
        ),
    )(
        latents,
        query_space,
        key_space,
        value_space,
        out_space,
        query_time,
        key_time,
        value_time,
        out_time,
        position_bias,
        bucket_table,
    )


def one_kernel(latents, *rest):
    frames, places, _ = latents.shape
    n = lax.axis_size(AXIS)
    limit = (rest[-1].shape[0] - 1) // 2
    fits = frames == 1 and n % 2 == 0 and places % (16 * n) == 0 and limit + n <= 256 and n <= limit
    return (kernel_body if fits else body)(latents, *rest)


def solution(mesh):
    in_specs = (P(("batch", "frame"), None, None), P(), P(), P(), P(), P(), P(), P(), P(), P(), P())
    out_specs = P(("batch", "frame"), None, None)
    return jax.shard_map(one_kernel, mesh=mesh, in_specs=in_specs, out_specs=out_specs, check_vma=False)
```

```python
import functools
import math

import jax
import jax.numpy as jnp
from jax import lax
from jax.experimental import pallas as pl
from jax.experimental.pallas import tpu as pltpu
from jax.sharding import PartitionSpec as P

HEADS = 8
HEAD_DIM = 80


EPS = 1e-05


def from_behind(x, axis, by):
    size = lax.axis_size(axis)
    pairs = [(i, i + by) for i in range(size) if 0 <= i + by < size]
    return lax.ppermute(x, axis, pairs)


def spread_2(block, axis, source):
    block = jnp.where(lax.axis_index(axis) == source, block, jnp.zeros_like(block))
    return lax.psum(block, axis)


def normalize(values):
    floats = values.astype(jnp.float32)
    average = jnp.mean(floats, axis=-1, keepdims=True)
    centred = floats - average
    spread = jnp.mean(centred * centred, axis=-1, keepdims=True)
    return (centred * lax.rsqrt(spread + EPS)).astype(jnp.bfloat16)


def project(rows, weight):
    lead = rows.shape[:-1]
    flat = rows.reshape(-1, rows.shape[-1])
    result = jnp.dot(flat, weight, preferred_element_type=jnp.float32)
    return result.reshape(lead + (weight.shape[1],)).astype(jnp.bfloat16)


def softmax_rows(scores):
    highest = jnp.max(scores, axis=-1, keepdims=True)
    powered = jnp.exp(scores - highest)
    return (powered / jnp.sum(powered, axis=-1, keepdims=True)).astype(jnp.bfloat16)


def temporal_attend(time_q, time_k, time_v, bias_rows):
    frames, places, channels = time_q.shape
    factor = 1.0 / math.sqrt(HEAD_DIM)
    block_rows = math.gcd(frames, 512)
    blocks = frames // block_rows
    limit = (bias_rows.shape[1] - 1) // 2
    key_rows = time_k.reshape(frames, places, HEADS, HEAD_DIM)
    value_rows = time_v.reshape(frames, places, HEADS, HEAD_DIM)
    columns = jnp.arange(frames, dtype=jnp.int32)

    def one_block(begin_row):
        query_rows = time_q.reshape(block_rows, places, HEADS, HEAD_DIM)
        row_ids = begin_row + jnp.arange(block_rows, dtype=jnp.int32)
        offsets = jnp.clip(columns[None, :] - row_ids[:, None], -limit, limit) + limit
        bias = bias_rows[:, offsets]
        scores = (
            jnp.einsum("iphe,jphe->phij", query_rows, key_rows, preferred_element_type=jnp.float32)
            * factor
            + bias[None]
        )
        weights = softmax_rows(scores)
        mixed = jnp.einsum(
            "phij,jphe->iphe", weights, value_rows, preferred_element_type=jnp.float32
        )
        return mixed.astype(jnp.bfloat16).reshape(block_rows, places, channels)

    results = lax.map(one_block, jnp.arange(blocks, dtype=jnp.int32) * block_rows)
    return results.reshape(frames, places, channels)


def squeeze_items(rows):
    return rows.reshape(rows.shape[0], rows.shape[2], rows.shape[3])


def body(
    latents,
    query_space,
    key_space,
    value_space,
    out_space,
    query_time,
    key_time,
    value_time,
    out_time,
    position_bias,
    bucket_table,
):
    frames, places, channels = latents.shape
    factor = 1.0 / math.sqrt(HEAD_DIM)
    normed = normalize(latents)
    space_q = project(normed, query_space)
    space_k = project(normed, key_space)
    space_v = project(normed, value_space)
    prior_pair = from_behind(jnp.stack([space_k[-1], space_v[-1]]), "frame", 1)
    first_pair = spread_2(jnp.stack([space_k[0], space_v[0]]), "frame", 0)
    prior_keys, prior_values = (prior_pair[0], prior_pair[1])
    first_keys, first_values = (first_pair[0], first_pair[1])
    is_first = lax.axis_index("frame") == 0
    prior_keys = jnp.where(is_first, first_keys, prior_keys)
    prior_values = jnp.where(is_first, first_values, prior_values)
    before_keys = jnp.concatenate([prior_keys[None], space_k[:-1]], axis=0)
    before_values = jnp.concatenate([prior_values[None], space_v[:-1]], axis=0)
    key_rows = jnp.concatenate([first_keys[None], before_keys], axis=1)
    value_rows = jnp.concatenate([first_values[None], before_values], axis=1)
    query_rows = space_q.reshape(frames, places, HEADS, HEAD_DIM)
    key_rows = key_rows.reshape(frames, 2 * places, HEADS, HEAD_DIM)
    value_rows = value_rows.reshape(frames, 2 * places, HEADS, HEAD_DIM)
    scores = (
        jnp.einsum("fqhe,fkhe->fhqk", query_rows, key_rows, preferred_element_type=jnp.float32)
        * factor
    )
    weights = softmax_rows(scores)
    space_mix = jnp.einsum(
        "fhqk,fkhe->fqhe", weights, value_rows, preferred_element_type=jnp.float32
    ).astype(jnp.bfloat16)
    space_out = jnp.dot(
        space_mix.reshape(-1, channels), out_space, preferred_element_type=jnp.float32
    ).reshape(frames, places, channels)
    after_space = (latents.astype(jnp.float32) + space_out).astype(jnp.bfloat16)
    normed_two = normalize(after_space)
    onehot = (
        bucket_table[:, None] == jnp.arange(position_bias.shape[1], dtype=jnp.int32)[None, :]
    ).astype(jnp.float32)
    bias_rows = jnp.dot(position_bias, onehot.T, precision=lax.Precision.HIGHEST)
    owners = lax.axis_size("frame")
    share = places // owners
    flat_rows = squeeze_items(
        lax.all_to_all(
            normed_two.reshape(frames, owners, share, channels),
            "frame",
            split_axis=1,
            concat_axis=0,
            tiled=True,
        )
    )
    mixed = temporal_attend(
        project(flat_rows, query_time),
        project(flat_rows, key_time),
        project(flat_rows, value_time),
        bias_rows,
    )
    gathered_mix = mixed[:, None]
    time_mix = lax.all_to_all(
        gathered_mix, "frame", split_axis=0, concat_axis=1, tiled=True
    ).reshape(frames, places, channels)
    time_out = jnp.dot(
        time_mix.reshape(-1, channels), out_time, preferred_element_type=jnp.float32
    ).reshape(frames, places, channels)
    return (after_space.astype(jnp.float32) + time_out).astype(jnp.bfloat16)


AXIS = "frame"
MESH = pl.DeviceIdType.MESH
LANES = 128
FAR_BELOW = -1e30
LOG2E = 1.4426950408889634


def windows(channels):
    spans = []
    for head in range(HEADS):
        begin, end = head * HEAD_DIM, (head + 1) * HEAD_DIM
        low = begin // LANES * LANES
        high = min(-(-end // LANES) * LANES, channels)
        spans.append((low, high, begin - low, end - low))
    return spans


def attend(q_ref, k_ref, v_ref, rows, scale, bias_ref):
    channels = q_ref.shape[-1]
    tiles = [None] * (channels // LANES)
    for head, (low, high, begin, end) in enumerate(windows(channels)):
        lane = lax.broadcasted_iota(jnp.int32, (rows.size, high - low), 1)
        inside = (lane >= begin) & (lane < end)
        query = q_ref[rows, low:high]
        query = jnp.where(inside, query, jnp.zeros_like(query))
        scores = lax.dot_general(
            query, k_ref[:, low:high], (((1,), (1,)), ((), ())), preferred_element_type=jnp.float32
        )
        if bias_ref is None:
            highest = jnp.max(scores, axis=-1, keepdims=True)
            powered = jnp.exp2((scores - highest) * (scale * LOG2E))
        else:
            scores = scores * scale + bias_ref[head, rows, :]
            highest = jnp.max(scores, axis=-1, keepdims=True)
            powered = jnp.exp2((scores - highest) * LOG2E)
        total = jnp.sum(powered, axis=-1, keepdims=True)
        mixed = jnp.dot(
            powered.astype(jnp.bfloat16), v_ref[:, low:high], preferred_element_type=jnp.float32
        )
        mixed = mixed * (1.0 / total)
        for at in range(low, high, LANES):
            part = mixed[:, at - low : at - low + LANES]
            keep = inside[:, at - low : at - low + LANES]
            old = tiles[at // LANES]
            tiles[at // LANES] = part if old is None else jnp.where(keep, part, old)
    return jnp.concatenate([t.astype(jnp.bfloat16) for t in tiles], axis=1)


def norm_rows(floats):
    average = jnp.mean(floats, axis=-1, keepdims=True)
    centred = floats - average
    spread = jnp.mean(centred * centred, axis=-1, keepdims=True)
    return (centred * lax.rsqrt(spread + EPS)).astype(jnp.bfloat16)


def matmul(rows, weight):
    return jnp.dot(rows, weight, preferred_element_type=jnp.float32)


def block_kernel(
    n,
    share,
    lat,
    *refs,
):
    weights, refs = refs[:8], refs[8:]
    bias_table, bucket_row, out = refs[:3]
    (
        x,
        w,
        first,
        prior,
        q,
        k,
        v,
        after,
        go,
        came,
        back_go,
        back_came,
        bias,
        pos_bias,
        buckets,
        x_sem,
        w_sem,
        t_sem,
        prior_sems,
        a_send,
        b_send,
        c_send,
        first_recv,
        go_send,
        go_recv,
        back_send,
        back_recv,
    ) = refs[3:]
    me = lax.axis_index(AXIS)
    places, channels = x.shape
    scale = 1.0 / math.sqrt(HEAD_DIM)
    other = lax.rem(me + 1, n)

    barrier = pltpu.get_barrier_semaphore()

    @pl.loop(1, n)
    def _(step):
        pl.semaphore_signal(
            barrier, inc=1, device_id={AXIS: lax.rem(me + step, n)}, device_id_type=MESH
        )

    own = pltpu.make_async_copy(lat.at[0], x, x_sem)
    own.start()
    tables = [
        pltpu.make_async_copy(bias_table, pos_bias, t_sem.at[0]),
        pltpu.make_async_copy(bucket_row, buckets, t_sem.at[1]),
    ]
    for table in tables:
        table.start()
    loads = [pltpu.make_async_copy(weights[i], w.at[i], w_sem.at[i]) for i in range(8)]
    for load in loads:
        load.start()

    pl.semaphore_wait(barrier, n - 1)

    def chunk(c):
        return lat.at[0, pl.ds(pl.multiple_of(c * share, share), share), :]

    def scatter(c):
        return pltpu.make_async_remote_copy(
            chunk(c), first.at[c], a_send.at[c], first_recv.at[c], {AXIS: c}, MESH
        )

    def gather(c, to):
        return pltpu.make_async_remote_copy(
            first.at[c], first.at[c], b_send.at[to], first_recv.at[c], {AXIS: to}, MESH
        )

    sibling = me + 1 - 2 * lax.rem(me, 2)

    def pair(c):
        return pltpu.make_async_remote_copy(
            first.at[c], first.at[c], c_send.at[c], first_recv.at[c], {AXIS: sibling}, MESH
        )

    send_prior = pltpu.make_async_remote_copy(
        lat.at[0], prior, prior_sems.at[0], prior_sems.at[1], {AXIS: other}, MESH
    )

    @pl.when(me == 0)
    def _():
        @pl.loop(1, n)
        def _(step):
            scatter(n - step).start()

    @pl.when(me < n - 1)
    def _():
        send_prior.start()

    own.wait()

    @pl.when(me == 0)
    def _():
        prior[...] = x[...]
        first[...] = x[...].reshape(n, share, channels)

    def took(c):
        pltpu.make_async_remote_copy(
            first.at[c], first.at[c], b_send.at[0], first_recv.at[c], {AXIS: other}, MESH
        ).wait_recv()

    @pl.when(me > 0)
    def _():
        took(me)

    @pl.loop(1, n // 2)
    def _(step):
        to = lax.rem(me + 2 * step, n)

        @pl.when(to != 0)
        def _():
            gather(me, to).start()

    @pl.when(sibling != 0)
    def _():
        pair(me).start()

    normed = norm_rows(x[...].astype(jnp.float32))
    loads[0].wait()
    q[...] = matmul(normed, w[0]).astype(jnp.bfloat16)

    @pl.loop(1, n // 2)
    def _(step):
        c = lax.rem(me + n - 2 * step, n)

        @pl.when(me > 0)
        def _():
            took(c)

        @pl.when(sibling != 0)
        def _():
            pair(c).start()

    @pl.when(me > 0)
    def _():
        pltpu.make_async_remote_copy(
            lat.at[0], prior, prior_sems.at[0], prior_sems.at[1], {AXIS: other}, MESH
        ).wait_recv()

    normed = norm_rows(prior[...].astype(jnp.float32))
    loads[1].wait()
    loads[2].wait()
    k[places:, :] = matmul(normed, w[1]).astype(jnp.bfloat16)
    v[places:, :] = matmul(normed, w[2]).astype(jnp.bfloat16)

    @pl.when(me > 0)
    def _():
        @pl.loop(0, n // 2)
        def _(step):
            took(2 * step + lax.rem(me + 1, 2))

    normed = norm_rows(first[...].reshape(places, channels).astype(jnp.float32))
    k[:places, :] = matmul(normed, w[1]).astype(jnp.bfloat16)
    v[:places, :] = matmul(normed, w[2]).astype(jnp.bfloat16)

    for i in range(3, 8):
        loads[i].wait()

    halves = 1
    size = places // halves

    def place(device):
        return device

    def to_owner(to):
        return pltpu.make_async_remote_copy(
            go.at[place(to)], came.at[me], go_send.at[to], go_recv.at[me], {AXIS: to}, MESH
        )

    def to_frame(to):
        return pltpu.make_async_remote_copy(
            back_go.at[place(to)],
            back_came.at[place(me)],
            back_send.at[to],
            back_recv.at[me],
            {AXIS: to},
            MESH,
        )

    def start_group(make, half):
        count = n // halves

        @pl.loop(0, count)
        def _(step):
            to = lax.rem(me + step, count)

            @pl.when(to != me)
            def _():
                make(to).start()

    def space_block(half):
        rows = pl.ds(pl.multiple_of(half * size, size), size)
        mix = attend(q, k, v, rows, scale, None)
        summed = x[rows, :].astype(jnp.float32) + matmul(mix, w[3])
        rounded = summed.astype(jnp.bfloat16)
        after[rows, :] = rounded
        go[pl.ds(half * (n // halves), n // halves)] = norm_rows(
            rounded.astype(jnp.float32)
        ).reshape(n // halves, share, channels)
        start_group(to_owner, half)

    pl.loop(0, halves)(space_block)

    came[pl.ds(me, 1)] = go[pl.ds(place(me), 1)]

    for table in tables:
        table.wait()

    onehot = (
        lax.broadcasted_iota(jnp.int32, (pos_bias.shape[1], 256), 0) == buckets[0:256].reshape(1, 256)
    ).astype(jnp.float32)
    by_offset = jnp.dot(
        pos_bias[...], onehot, precision=lax.Precision.HIGHEST, preferred_element_type=jnp.float32
    )
    limit = (buckets.shape[0] - 1) // 2
    wide = 2 * n * share
    pick = (
        lax.broadcasted_iota(jnp.int32, (256, wide), 0)
        == lax.broadcasted_iota(jnp.int32, (256, wide), 1) // share + (limit - (n - 1))
    ).astype(jnp.float32)
    spread = jnp.dot(
        by_offset, pick, precision=lax.Precision.HIGHEST, preferred_element_type=jnp.float32
    )
    same = lax.broadcasted_iota(jnp.int32, (share, n * share), 0) == lax.rem(
        lax.broadcasted_iota(jnp.int32, (share, n * share), 1), share
    )
    order = list(range(n))
    for block, i in enumerate(order):
        begin = (n - 1 - i) * share
        line = spread[:, begin : begin + n * share]
        for head in range(HEADS):
            bias[head, block * share : (block + 1) * share, :] = jnp.where(
                same, line[head : head + 1, :], FAR_BELOW
            )

    @pl.loop(1, n)
    def _(step):
        c = lax.rem(me + step, n)
        pltpu.make_async_remote_copy(
            came.at[c], came.at[c], go_send.at[c], go_recv.at[c], {AXIS: c}, MESH
        ).wait_recv()

    rows = came[...].reshape(n * share, channels)
    ordered = jnp.concatenate([came[i] for i in order], axis=0)
    q[...] = matmul(ordered, w[4]).astype(jnp.bfloat16)
    k[:places, :] = matmul(rows, w[5]).astype(jnp.bfloat16)
    v[:places, :] = matmul(rows, w[6]).astype(jnp.bfloat16)

    def time_block(half):
        rows = pl.ds(pl.multiple_of(half * size, size), size)
        mix = attend(q, k.at[:places], v.at[:places], rows, scale, bias)
        back_go[pl.ds(half * (n // halves), n // halves)] = mix.reshape(
            n // halves, share, channels
        )
        start_group(to_frame, half)

    pl.loop(0, halves)(time_block)

    back_came[pl.ds(place(me), 1)] = back_go[pl.ds(place(me), 1)]

    @pl.loop(1, n)
    def _(step):
        c = lax.rem(me + step, n)
        pltpu.make_async_remote_copy(
            back_came.at[place(c)],
            back_came.at[place(c)],
            back_send.at[c],
            back_recv.at[c],
            {AXIS: c},
            MESH,
        ).wait_recv()

    mix = back_came[...].reshape(places, channels)
    out[0] = (after[...].astype(jnp.float32) + matmul(mix, w[7])).astype(jnp.bfloat16)

    @pl.when(me == 0)
    def _():
        @pl.loop(1, n)
        def _(step):
            scatter(n - step).wait_send()

    @pl.when(me < n - 1)
    def _():
        send_prior.wait_send()

    @pl.loop(1, n // 2)
    def _(step):
        to = lax.rem(me + 2 * step, n)

        @pl.when(to != 0)
        def _():
            gather(me, to).wait_send()

    @pl.when(sibling != 0)
    def _():
        @pl.loop(0, n // 2)
        def _(step):
            pair(lax.rem(me + 2 * step, n)).wait_send()

    @pl.loop(1, n)
    def _(step):
        c = lax.rem(me + step, n)
        to_owner(c).wait_send()
        to_frame(c).wait_send()


def kernel_body(
    latents,
    query_space,
    key_space,
    value_space,
    out_space,
    query_time,
    key_time,
    value_time,
    out_time,
    position_bias,
    bucket_table,
):
    _, places, channels = latents.shape
    n = lax.axis_size(AXIS)
    share = places // n
    rows = n * share
    bf16 = jnp.bfloat16
    anywhere = pl.BlockSpec(memory_space=pltpu.HBM)
    vmem = pl.BlockSpec(memory_space=pltpu.VMEM)
    blocks = pltpu.VMEM((n, share, channels), bf16)
    plane = pltpu.VMEM((places, channels), bf16)
    dma = pltpu.SemaphoreType.DMA
    return pl.pallas_call(
        functools.partial(block_kernel, n, share),
        out_shape=jax.ShapeDtypeStruct(latents.shape, bf16),
        in_specs=[anywhere] * 11,
        out_specs=vmem,
        scratch_shapes=[
            plane,
            pltpu.VMEM((8, channels, channels), bf16),
            blocks,
            plane,
            plane,
            pltpu.VMEM((2 * places, channels), bf16),
            pltpu.VMEM((2 * places, channels), bf16),
            plane,
            blocks,
            blocks,
            blocks,
            blocks,
            pltpu.VMEM((HEADS, rows, rows), jnp.float32),
            pltpu.VMEM(position_bias.shape, jnp.float32),
            pltpu.VMEM(bucket_table.shape, jnp.int32),
            dma,
            dma((8,)),
            dma((2,)),
            dma((2,)),
            dma((n,)),
            dma((n,)),
            dma((n,)),
            dma((n,)),
            dma((n,)),
            dma((n,)),
            dma((n,)),
            dma((n,)),
        ],
        compiler_params=pltpu.CompilerParams(
            collective_id=0, has_side_effects=True, vmem_limit_bytes=63 * 1024 * 1024
        ),
    )(
        latents,
        query_space,
        key_space,
        value_space,
        out_space,
        query_time,
        key_time,
        value_time,
        out_time,
        position_bias,
        bucket_table,
    )


def one_kernel(latents, *rest):
    frames, places, _ = latents.shape
    n = lax.axis_size(AXIS)
    limit = (rest[-1].shape[0] - 1) // 2
    fits = frames == 1 and n % 2 == 0 and places % (16 * n) == 0 and limit + n <= 256 and n <= limit
    return (kernel_body if fits else body)(latents, *rest)


def solution(mesh):
    in_specs = (P(("batch", "frame"), None, None), P(), P(), P(), P(), P(), P(), P(), P(), P(), P())
    out_specs = P(("batch", "frame"), None, None)
    return jax.shard_map(one_kernel, mesh=mesh, in_specs=in_specs, out_specs=out_specs, check_vma=False)
```
